32 devices in a mesh: recv: 8 (over z, x), src: 4 (over y, core).
Axes of the slice: x: 2, y: 2, z: 4, core: 2. Of those that a mesh axis runs over, the one named last changes fastest.
Arguments:
- interactions: int32 [3, 3072], P(None, ('recv', 'src')), may hold values from 0 to 255, as said below
- list_lengths: int32 [32], P(('recv', 'src')), may hold values from 48 to 96, as said below
- kernels: float32 [128, 128, 16, 128], P(('recv', 'src')), may hold values from -0.0210316469 to 0.0210316469
- prestress: float32 [256, 128], P(('recv', 'src')), may hold values from 2 to 3
- friction: float32 [256, 128], P(('recv', 'src')), may hold values from 0.2 to 0.5
- load_rate: float32 [256, 128], P(('recv', 'src')), may hold values from 0.04 to 0.08
Outputs:
- slip_rates: float32 [256, 96, 128], P(('recv', 'src'))
The draws below stay inside these ranges and needn't reach their ends.
Inputs may be any that keep to these rules, and one draw needn't show every extreme that they name: `interactions`: column e belongs to device block g = e // 96, g = i * 4 + j. Its receiver patch lies in [i * 4 * 8, (i + 1) * 4 * 8); its source patch p satisfies (p // 8) mod 4 == j; its owner is p // 32; its lag offset lies in [32, 48]. The entries of one block name at most 1 distinct source patches of one owner, and in every draw some owner supplies exactly that many distinct source patches to every block. `list_lengths`: some device's list is full and some device's list holds exactly half, in every draw.
All inputs are finite; a program needn't handle non-finite values.
Results may differ from the reference program's by a relative error of at most 0.0003.
Values sent between devices are 32-bit elements; how exact they have to be, the bound alone decides.
No kernel may reach another device: no remote copies, remote signals or barrier semaphores. Data moves between devices by JAX's collectives and lax.ppermute only.
A program may use at most 128 MiB of HBM per device.

```python
import math
import jax
import jax.numpy as jnp
from jax import lax

PE = 128
LAGS = 16
BLOCK = 32
BLOCKS = 3
NEWTON = 4
PATCH_DEV = 8
KER_DEV = 4
ENT_KER = 24
ENT_DEV = 96
PEER_CAP = 1
OWNERS = 8
STRIPS = 4
PATCHES = 256
KERNEL_TOTAL = 128


def draw_interactions(key, part):
    devices = OWNERS * STRIPS
    key_recv, key_src, key_lag, key_hot, key_weight, key_score, key_order = jax.random.split(jax.random.fold_in(key, 11), 7)
    device_ids = jnp.arange(devices, dtype=jnp.int32)
    group_idx = device_ids // STRIPS
    strip_idx = device_ids % STRIPS
    receivers = group_idx[:, None] * (STRIPS * PATCH_DEV) + jax.random.randint(key_recv, (devices, ENT_DEV), 0, STRIPS * PATCH_DEV)
    slot_count = OWNERS * PEER_CAP
    slot_ids = jnp.arange(slot_count, dtype=jnp.int32)
    slot_owner = slot_ids // PEER_CAP
    slot_rank = slot_ids % PEER_CAP
    starting_patch = jax.random.randint(key_src, (devices, OWNERS), 0, PATCH_DEV)
    slot_local = (starting_patch[:, slot_owner] + slot_rank[None, :]) % PATCH_DEV
    slot_patch = (slot_owner[None, :] * STRIPS + strip_idx[:, None]) * PATCH_DEV + slot_local
    hot_owner = jax.random.randint(key_hot, (), 0, OWNERS)
    owner_weight = jax.random.randint(key_weight, (OWNERS,), 1, 5)
    owner_weight = jnp.where(jnp.arange(OWNERS, dtype=jnp.int32) == hot_owner, 16, owner_weight)
    cumulative = jnp.cumsum(owner_weight[slot_owner])
    total_weight = cumulative[-1]
    picks = jax.random.randint(key_score, (devices, ENT_DEV), 0, 2 ** 30) % total_weight
    chosen = jnp.sum((cumulative[None, None, :] <= picks[:, :, None]).astype(jnp.int32), axis=2)
    forced = hot_owner * PEER_CAP + jnp.arange(PEER_CAP, dtype=jnp.int32)
    chosen = chosen.at[:, :PEER_CAP].set(jnp.broadcast_to(forced[None, :], (devices, PEER_CAP)))
    order_keys = jax.random.split(key_order, devices)
    chosen = jax.vmap(jax.random.permutation)(order_keys, chosen)
    sources = jnp.take_along_axis(slot_patch, chosen, axis=1)
    delays = jax.random.randint(key_lag, (devices, ENT_DEV), BLOCK, 2 * BLOCK - LAGS + 1)
    return jnp.stack([receivers.reshape(-1), sources.reshape(-1), delays.reshape(-1)]).astype(jnp.int32)


def draw_list_lengths(key, part):
    devices = OWNERS * STRIPS
    key_len, key_perm = jax.random.split(jax.random.fold_in(key, 23), 2)
    lengths = jax.random.randint(key_len, (devices,), ENT_DEV // 2, ENT_DEV + 1)
    shuffled = jax.random.permutation(key_perm, devices)
    lengths = lengths.at[shuffled[0]].set(ENT_DEV).at[shuffled[1]].set(ENT_DEV // 2)
    return lengths.astype(jnp.int32)


def draw_kernels(key, part):
    key_base, key_gain = jax.random.split(jax.random.fold_in(key, 37), 2)
    full_shape = (KERNEL_TOTAL, PE, LAGS, PE)
    spread = float(8 * LAGS * PE * ENT_DEV // PATCH_DEV) ** (-0.5)
    base = jnp.clip(jax.random.normal(key_base, full_shape, jnp.float32), -6.0, 6.0) * spread
    gains = jax.random.uniform(key_gain, (KERNEL_TOTAL, PE, 1, PE), jnp.float32, 0.5, 1.5)
    centred = jnp.arange(LAGS, dtype=jnp.float32) - 0.5 * (LAGS - 1)
    bend = centred * centred
    bend = bend - jnp.mean(bend)
    bend = bend / jnp.max(jnp.abs(bend))
    fourth = jnp.sum(centred ** 4) / jnp.sum(centred ** 2)
    twist = centred ** 3 - fourth * centred
    twist = twist / jnp.max(jnp.abs(twist))
    profile = 0.002 * bend + 0.003 * twist
    return base + gains * profile[None, None, :, None]


def shard_levels(own_key, extent, cuts, least, top_value):
    factor_of = 1.0
    for position, parts in cuts:
        steps = jax.random.uniform(jax.random.fold_in(jax.random.fold_in(own_key, 6), position), (parts,), jnp.float32, least / len(cuts), top_value / len(cuts))
        factor_of = factor_of * jnp.repeat(jnp.exp(steps), extent[position] // parts).reshape((-1,) + (1,) * (len(extent) - 1 - position))
    return factor_of


def setup_inputs(seed: int = 0) -> dict:
    splits = jax.random.split(jax.random.key(seed), 7)
    return {
        "interactions": draw_interactions(jax.random.fold_in(splits[6], 71), 0),
        "list_lengths": draw_list_lengths(jax.random.fold_in(splits[6], 71), 0),
        "kernels": draw_kernels(jax.random.fold_in(splits[6], 71), 0),
        "prestress": jnp.clip(2.0 + 1.0 * jax.random.uniform(splits[3], (PATCHES, PE), jnp.float32) ** shard_levels(splits[3], (PATCHES, PE), ((0, 32),), -0.2, 0.2), 2.0, 3.0),
        "friction": jnp.clip(jnp.exp(math.log(0.5) - 0.9162907 * jax.random.uniform(splits[4], (PATCHES, PE), jnp.float32) ** shard_levels(splits[4], (PATCHES, PE), ((0, 32),), -0.2, 0.2)), 0.2, 0.5),
        "load_rate": jnp.clip(jnp.exp(math.log(0.08) - 0.6931472 * jax.random.uniform(splits[5], (PATCHES, PE), jnp.float32) ** shard_levels(splits[5], (PATCHES, PE), ((0, 32),), -0.2, 0.2)), 0.04, 0.08),
    }


damping = 0.5

def inverse_sinh(values):
    magnitude = jnp.abs(values)
    result = jnp.log(magnitude + jnp.sqrt(1.0 + magnitude * magnitude))
    return jnp.where(values < 0, -result, result)

def friction_solve(drive, friction):
    rates = jnp.zeros_like(drive)
    for newton_step in range(NEWTON):
        misfit = damping * rates + friction * inverse_sinh(rates) - drive
        slope_now = damping + friction * lax.rsqrt(1.0 + rates * rates)
        rates = rates - misfit / slope_now
    return rates

def lagged_stack(windows, delays):

    def cut_window(window, delay):
        return lax.dynamic_slice_in_dim(window, 2 * BLOCK - delay - (LAGS - 1), BLOCK + LAGS - 1, 0)
    segments = jax.vmap(cut_window)(windows, delays)
    pieces = [segments[:, LAGS - 1 - lag_idx:LAGS - 1 - lag_idx + BLOCK] for lag_idx in range(LAGS)]
    return jnp.stack(pieces, axis=2)

def interaction_stress(window_all, interactions, list_lengths, kernels):

    def one_device(total, device):
        entries = lax.dynamic_slice_in_dim(interactions, device * ENT_DEV, ENT_DEV, 1)
        windows = jnp.take(window_all, entries[1], axis=0)
        stacked_rows = lagged_stack(windows, entries[2]).reshape(KER_DEV, ENT_KER * BLOCK, LAGS * PE)
        kernel_matrices = lax.dynamic_slice_in_dim(kernels, device * KER_DEV, KER_DEV, 0).reshape(KER_DEV, PE, LAGS * PE)
        stress_terms = jnp.einsum('svf,sif->svi', stacked_rows, kernel_matrices, precision=lax.Precision.HIGHEST)
        stress_terms = stress_terms.reshape(ENT_DEV, BLOCK, PE)
        live = (jnp.arange(ENT_DEV, dtype=jnp.int32) < list_lengths[device]).astype(jnp.float32)
        return (total.at[entries[0]].add(stress_terms * live[:, None, None]), None)
    start = jnp.zeros((PATCHES, BLOCK, PE), jnp.float32)
    total, unused = lax.scan(one_device, start, jnp.arange(OWNERS * STRIPS, dtype=jnp.int32))
    return total

def reference(interactions, list_lengths, kernels, prestress, friction, load_rate):
    zeros_front = jnp.zeros((PATCHES, 2 * BLOCK, PE), jnp.float32)
    finished_blocks = []
    for block_idx in range(BLOCKS):
        if block_idx == 0:
            stress = jnp.zeros((PATCHES, BLOCK, PE), jnp.float32)
        else:
            padded = jnp.concatenate([zeros_front] + finished_blocks, axis=1)
            window_all = padded[:, block_idx * BLOCK:block_idx * BLOCK + 2 * BLOCK]
            stress = interaction_stress(window_all, interactions, list_lengths, kernels)
        times = (block_idx * BLOCK + 1 + jnp.arange(BLOCK, dtype=jnp.int32)).astype(jnp.float32)
        drive = prestress[:, None, :] + load_rate[:, None, :] * times[None, :, None] + stress
        finished_blocks.append(friction_solve(drive, friction[:, None, :]))
    return jnp.concatenate(finished_blocks, axis=1)
```

```python
import functools

import jax
import jax.numpy as jnp
from jax import lax
from jax.experimental import pallas as pl
from jax.experimental.pallas import tpu as pltpu
from jax.sharding import PartitionSpec as P

BLOCK = 32
BLOCKS = 3
NEWTON = 4
damping = 0.5
VMEM = pl.BlockSpec(memory_space=pltpu.VMEM)
SMEM = pl.BlockSpec(memory_space=pltpu.SMEM)


def friction_solve(drive, friction):
    rates = drive / (damping + friction)
    for newton_step in range(NEWTON - 1):
        squares = 1.0 + rates * rates
        inverse_root = lax.rsqrt(squares)
        magnitude = jnp.log(jnp.abs(rates) + squares * inverse_root)
        inverse_sinh = jnp.where(rates < 0, -magnitude, magnitude)
        misfit = damping * rates + friction * inverse_sinh - drive
        rates = rates - misfit / (damping + friction * inverse_root)
    return rates


def times_of(block_idx, width):
    steps = lax.broadcasted_iota(jnp.int32, (BLOCK, width), 0)
    return (steps + (block_idx * BLOCK + 1)).astype(jnp.float32)


def split(values):
    high = values.astype(jnp.bfloat16)
    return high, (values - high.astype(jnp.float32)).astype(jnp.bfloat16)


def weights_kernel(kernel_ref, high_ref, low_ref):
    lag_count, width = kernel_ref.shape[2], kernel_ref.shape[3]
    for lag in range(lag_count):
        high, low = split(kernel_ref[0, :, lag, :].T)
        high_ref[lag * width : (lag + 1) * width, :] = high
        low_ref[lag * width : (lag + 1) * width, :] = low


def first_block_kernel(prestress_ref, friction_ref, load_ref, out_ref):
    patch_count, width = prestress_ref.shape
    times = times_of(0, width)
    for patch in range(patch_count):
        row = pl.ds(patch, 1)
        drive = prestress_ref[row, :] + load_ref[row, :] * times
        out_ref[patch] = friction_solve(drive, jnp.broadcast_to(friction_ref[row, :], drive.shape))


def convolve_and_route(
    window, stacked, responses, sums, high_ref, low_ref, table_ref, keep_ref, send_ref
):
    slots, span, width = window.shape
    history = span - BLOCK
    ker_count = responses.shape[0]
    lag_count = high_ref.shape[0] // width
    chunk = stacked.shape[0] // (2 * BLOCK)
    rows = chunk * BLOCK

    def one_chunk(chunk_idx, carry):
        first = chunk_idx * chunk
        for lag in range(lag_count):
            for slot in range(chunk):
                high, low = split(window[first + slot, history - lag : history - lag + BLOCK, :])
                cols = slice(lag * width, (lag + 1) * width)
                stacked[slot * BLOCK : (slot + 1) * BLOCK, cols] = high
                stacked[rows + slot * BLOCK : rows + (slot + 1) * BLOCK, cols] = low
        both = jnp.dot(stacked[...], high_ref[...], preferred_element_type=jnp.float32)
        rest = jnp.dot(stacked[:rows, :], low_ref[...], preferred_element_type=jnp.float32)
        total = both[:rows] + both[rows:] + rest
        for ker in range(ker_count):
            for slot in range(chunk):
                responses[ker, first + slot, history:, :] = total[
                    slot * BLOCK : (slot + 1) * BLOCK, ker * width : (ker + 1) * width
                ]
        return carry

    chunks = slots // chunk
    if chunks == 1:
        one_chunk(0, 0)
    else:
        lax.fori_loop(0, chunks, one_chunk, 0)

    per_kernel = table_ref.shape[1] // ker_count
    for ker in range(ker_count):
        sums[ker][...] = jnp.zeros_like(sums[ker])
    for entry in range(per_kernel):
        for ker in range(ker_count):
            idx = ker * per_kernel + entry
            place = table_ref[0, idx]
            sums[ker][place] = (
                sums[ker][place]
                + responses[ker, table_ref[1, idx], pl.ds(table_ref[2, idx], BLOCK), :]
            )
    half = keep_ref.shape[0]
    for place in range(2 * half):
        total = sums[0][place]
        for ker in range(1, ker_count):
            total = total + sums[ker][place]
        if place < half:
            keep_ref[place] = total
        else:
            send_ref[place - half] = total


def first_stress_kernel(
    wanted_ref, table_ref, params_ref, high_ref, low_ref,
    keep_ref, send_ref, rates_tail_ref, responses_tail_ref,
    window, stacked, responses, *sums,
):
    slots, span, width = window.shape
    history = span - BLOCK
    patch_count = (params_ref.shape[1] - 1) // 3
    times = times_of(0, width)
    for ker in range(responses.shape[0]):
        responses[ker, :, :history, :] = jnp.zeros((slots, history, width), jnp.float32)

    def one_slot(slot):
        patch = wanted_ref[slot]
        drive = (
            params_ref[slot, pl.ds(patch, 1), :]
            + params_ref[slot, pl.ds(2 * patch_count + patch, 1), :] * times
        )
        friction = jnp.broadcast_to(
            params_ref[slot, pl.ds(patch_count + patch, 1), :], drive.shape
        )
        window[slot, :history, :] = jnp.zeros((history, width), jnp.float32)
        window[slot, history:, :] = friction_solve(drive, friction)

    if slots <= 8:
        for slot in range(slots):
            one_slot(slot)
    else:
        pl.loop(0, slots)(one_slot)
    convolve_and_route(
        window, stacked, responses, sums, high_ref, low_ref, table_ref, keep_ref, send_ref
    )
    rates_tail_ref[...] = window[:, BLOCK:, :]
    responses_tail_ref[...] = responses[:, :, BLOCK:, :]


def next_stress_kernel(
    table_ref, rates_ref, rates_tail_ref, responses_tail_ref, high_ref, low_ref,
    keep_ref, send_ref,
    window, stacked, responses, *sums,
):
    history = window.shape[1] - BLOCK
    window[:, :history, :] = rates_tail_ref[...]
    window[:, history:, :] = rates_ref[...]
    responses[:, :, :history, :] = responses_tail_ref[...]
    convolve_and_route(
        window, stacked, responses, sums, high_ref, low_ref, table_ref, keep_ref, send_ref
    )


def solve_patch(block_idx, patch, prestress_ref, friction_ref, load_ref, kept_ref, came_ref):
    width = prestress_ref.shape[1]
    row = pl.ds(patch, 1)
    stress = kept_ref[patch] + came_ref[patch]
    drive = prestress_ref[row, :] + load_ref[row, :] * times_of(block_idx, width) + stress
    return friction_solve(drive, jnp.broadcast_to(friction_ref[row, :], drive.shape))


def middle_block_kernel(
    asked_ref, prestress_ref, friction_ref, load_ref, kept_ref, came_ref, rates_ref, outgoing_ref
):
    for patch in range(prestress_ref.shape[0]):
        rates_ref[patch] = solve_patch(
            1, patch, prestress_ref, friction_ref, load_ref, kept_ref, came_ref
        )

    def one_slot(slot):
        outgoing_ref[slot] = rates_ref[asked_ref[slot]]

    slots = outgoing_ref.shape[0]
    if slots <= 8:
        for slot in range(slots):
            one_slot(slot)
    else:
        pl.loop(0, slots)(one_slot)


def last_block_kernel(
    prestress_ref, friction_ref, load_ref, kept_ref, came_ref, first_ref, second_ref, out_ref
):
    for patch in range(prestress_ref.shape[0]):
        out_ref[patch, :BLOCK, :] = first_ref[patch]
        out_ref[patch, BLOCK : 2 * BLOCK, :] = second_ref[patch]
        out_ref[patch, 2 * BLOCK :, :] = solve_patch(
            2, patch, prestress_ref, friction_ref, load_ref, kept_ref, came_ref
        )


def local(interactions, list_lengths, kernels, prestress, friction, load_rate):
    n_recv = lax.axis_size("recv")
    n_src = lax.axis_size("src")
    recv_idx = lax.axis_index("recv")
    src_idx = lax.axis_index("src")
    ent_count = interactions.shape[1]
    ker_count, width, lag_count, _ = kernels.shape
    patch_count = prestress.shape[0]
    group_rows = n_src * patch_count
    bits = n_src.bit_length() - 1
    assert n_src == 1 << bits and bits > 0

    owners = interactions[1] // group_rows
    local_patch = interactions[1] % patch_count
    slot_ids = jnp.arange(n_recv, dtype=jnp.int32)
    wanted = jnp.max(jnp.where(slot_ids[:, None] == owners[None, :], local_patch[None, :], 0), axis=1)
    params = jnp.concatenate([prestress, friction, load_rate], axis=0)
    outgoing = jnp.concatenate(
        [
            jnp.broadcast_to(params[None], (n_recv,) + params.shape),
            jnp.broadcast_to(wanted.astype(jnp.float32)[:, None, None], (n_recv, 1, width)),
        ],
        axis=1,
    )
    received = lax.all_to_all(outgoing, "recv", split_axis=0, concat_axis=0, tiled=True)
    asked = received[:, -1, 0].astype(jnp.int32)

    receivers = interactions[0] - recv_idx * group_rows
    distance = (receivers // patch_count) ^ src_idx
    place = jnp.zeros_like(distance)
    for bit in range(bits):
        place = place | (((distance >> bit) & 1) << (bits - 1 - bit))
    entry_numbers = jnp.arange(ent_count, dtype=jnp.int32)
    place = jnp.where(
        entry_numbers < list_lengths[0], place * patch_count + receivers % patch_count, group_rows
    )
    table = jnp.stack([place, owners, BLOCK + lag_count - interactions[2]])

    f32, bf16 = jnp.float32, jnp.bfloat16
    taps = lag_count * width
    high, low = pl.pallas_call(
        weights_kernel,
        grid=(ker_count,),
        in_specs=[pl.BlockSpec((1, width, lag_count, width), lambda k: (k, 0, 0, 0))],
        out_specs=[pl.BlockSpec((taps, width), lambda k: (0, k))] * 2,
        out_shape=[jax.ShapeDtypeStruct((taps, ker_count * width), bf16)] * 2,
        name="weights",
    )(kernels)
    first_rates = pl.pallas_call(
        first_block_kernel,
        in_specs=[VMEM] * 3,
        out_specs=VMEM,
        out_shape=jax.ShapeDtypeStruct((patch_count, BLOCK, width), f32),
        name="first_block",
    )(prestress, friction, load_rate)

    half = jax.ShapeDtypeStruct((group_rows // 2, BLOCK, width), f32)
    rates_tail = jax.ShapeDtypeStruct((n_recv, lag_count, width), f32)
    responses_tail = jax.ShapeDtypeStruct((ker_count, n_recv, lag_count, width), f32)
    chunk = min(8, n_recv)
    scratch = [
        pltpu.VMEM((n_recv, lag_count + BLOCK, width), f32),
        pltpu.VMEM((2 * chunk * BLOCK, taps), bf16),
        pltpu.VMEM((ker_count, n_recv, lag_count + BLOCK, width), f32),
    ] + [pltpu.VMEM((group_rows + 1, BLOCK, width), f32)] * ker_count

    def reduce_scatter(kept, sent):
        for bit in range(bits):
            pairs = [(i, i ^ (1 << bit)) for i in range(n_src)]
            came = lax.ppermute(sent, "src", pairs)
            if bit == bits - 1:
                return kept, came
            quarter = kept.shape[0] // 2
            sent = kept[quarter:] + came[quarter:]
            kept = kept[:quarter] + came[:quarter]

    kept, sent, rates_tail, responses_tail = pl.pallas_call(
        first_stress_kernel,
        in_specs=[SMEM, SMEM, VMEM, VMEM, VMEM],
        out_specs=[VMEM] * 4,
        out_shape=[half, half, rates_tail, responses_tail],
        scratch_shapes=scratch,
        name="first_stress",
    )(wanted, table, received, high, low)
    kept, came = reduce_scatter(kept, sent)
    second_rates, outgoing = pl.pallas_call(
        middle_block_kernel,
        in_specs=[SMEM] + [VMEM] * 5,
        out_specs=[VMEM] * 2,
        out_shape=[
            jax.ShapeDtypeStruct((patch_count, BLOCK, width), f32),
            jax.ShapeDtypeStruct((n_recv, BLOCK, width), f32),
        ],
        name="middle_block",
    )(asked, prestress, friction, load_rate, kept, came)
    rates = lax.all_to_all(outgoing, "recv", split_axis=0, concat_axis=0, tiled=True)
    kept, sent = pl.pallas_call(
        next_stress_kernel,
        in_specs=[SMEM] + [VMEM] * 5,
        out_specs=[VMEM] * 2,
        out_shape=[half, half],
        scratch_shapes=scratch,
        name="next_stress",
    )(table, rates, rates_tail, responses_tail, high, low)
    kept, came = reduce_scatter(kept, sent)
    return pl.pallas_call(
        last_block_kernel,
        in_specs=[VMEM] * 7,
        out_specs=VMEM,
        out_shape=jax.ShapeDtypeStruct((patch_count, BLOCKS * BLOCK, width), f32),
        name="last_block",
    )(prestress, friction, load_rate, kept, came, first_rates, second_rates)


def solution(mesh):
    in_specs = (
        P(None, ("recv", "src")),
        P(("recv", "src")),
        P(("recv", "src"), None, None, None),
        P(("recv", "src"), None),
        P(("recv", "src"), None),
        P(("recv", "src"), None),
    )
    out_specs = P(("recv", "src"), None, None)
    return jax.shard_map(local, mesh=mesh, in_specs=in_specs, out_specs=out_specs, check_vma=False)
```

```python
import functools

import jax
import jax.numpy as jnp
from jax import lax
from jax.experimental import pallas as pl
from jax.experimental.pallas import tpu as pltpu
from jax.sharding import PartitionSpec as P

BLOCK = 32
BLOCKS = 3
NEWTON = 4
damping = 0.5
def grant(mib):
    return pltpu.CompilerParams(vmem_limit_bytes=mib * 2**20)


VMEM = pl.BlockSpec(memory_space=pltpu.VMEM)
SMEM = pl.BlockSpec(memory_space=pltpu.SMEM)
HBM = pl.BlockSpec(memory_space=pltpu.HBM)


def friction_solve(drive, friction):
    rates = drive / (damping + friction)
    for newton_step in range(NEWTON - 1):
        squares = 1.0 + rates * rates
        inverse_root = lax.rsqrt(squares)
        magnitude = jnp.log(jnp.abs(rates) + squares * inverse_root)
        inverse_sinh = jnp.where(rates < 0, -magnitude, magnitude)
        misfit = damping * rates + friction * inverse_sinh - drive
        rates = rates - misfit / (damping + friction * inverse_root)
    return rates


def times_of(block_idx, width):
    steps = lax.broadcasted_iota(jnp.int32, (BLOCK, width), 0)
    return (steps + (block_idx * BLOCK + 1)).astype(jnp.float32)


def split(values):
    high = values.astype(jnp.bfloat16)
    return high, (values - high.astype(jnp.float32)).astype(jnp.bfloat16)


def wanted_patches(interactions_ref, slots, patch_count):
    sources = interactions_ref[pl.ds(1, 1), :]
    owners = lax.broadcasted_iota(jnp.int32, (slots, sources.shape[1]), 0)
    first = (owners * lax.axis_size("src") + lax.axis_index("src")) * patch_count
    offset = sources - first
    inside = (offset >= 0) & (offset < patch_count)
    wanted = jnp.max(jnp.where(inside, offset, 0).astype(jnp.float32), axis=1, keepdims=True)
    return owners, inside, wanted


def pack_kernel(interactions_ref, prestress_ref, friction_ref, load_ref, out_ref):
    slots, rows, width = out_ref.shape
    patch_count = prestress_ref.shape[0]
    wanted = wanted_patches(interactions_ref, slots, patch_count)[2]
    wanted = jnp.broadcast_to(wanted, (slots, width))
    for field, ref in enumerate((prestress_ref, friction_ref, load_ref)):
        out_ref[:, field * patch_count : (field + 1) * patch_count, :] = jnp.broadcast_to(
            ref[...][None], (slots, patch_count, width)
        )
    for slot in range(slots):
        out_ref[slot, rows - 1 :, :] = wanted[slot : slot + 1, :]


def split_lag(lag, raw, first, halves):
    ker_count, width = raw.shape[0], raw.shape[3]
    rows = slice(lag * width, (lag + 1) * width)
    for ker in range(ker_count):
        split_tile(raw[ker, :, first + lag, :], ker, rows, halves)


def split_tile(tile, ker, rows, halves):
    halves[ker, rows, :], halves[halves.shape[0] // 2 + ker, rows, :] = split(tile.T)


def prepare_kernel(
    patch_count, lengths_ref, interactions_ref, kernel_ref, halves, table_ref, wanted_ref,
    interactions, raw, list_sem, sems,
):
    ker_count, _, lag_count, width = raw.shape
    early = halves.shape[1] // width
    loads = [
        pltpu.make_async_copy(kernel_ref.at[ker], raw.at[ker], sems.at[ker])
        for ker in range(ker_count)
    ]
    list_load = pltpu.make_async_copy(interactions_ref, interactions, list_sem)
    list_load.start()
    for copy in loads:
        copy.start()
    list_load.wait()

    slots = wanted_ref.shape[0]
    owners, inside, wanted = wanted_patches(interactions, slots, patch_count)
    wanted_ref[...] = jnp.broadcast_to(wanted, wanted_ref.shape)
    n_src = lax.axis_size("src")
    group_rows = n_src * patch_count
    receivers = interactions[pl.ds(0, 1), :] - lax.axis_index("recv") * group_rows
    strips = jnp.zeros_like(receivers)
    for other in range(1, n_src):
        strips = strips + (receivers >= other * patch_count).astype(jnp.int32)
    distance = strips ^ lax.axis_index("src")
    bits = n_src.bit_length() - 1
    order = jnp.zeros_like(distance)
    for bit in range(bits):
        order = order | (((distance >> bit) & 1) << (bits - 1 - bit))
    place = order * patch_count + receivers - strips * patch_count
    live = lax.broadcasted_iota(jnp.int32, place.shape, 1) < lengths_ref[0]
    table_ref[pl.ds(0, 1), :] = jnp.where(live, place, group_rows)
    table_ref[pl.ds(1, 1), :] = jnp.max(
        jnp.where(inside, owners, 0).astype(jnp.float32), axis=0, keepdims=True
    ).astype(jnp.int32)
    table_ref[pl.ds(2, 1), :] = BLOCK + lag_count - interactions[pl.ds(2, 1), :]

    for ker in range(ker_count):
        loads[ker].wait()
        for lag in range(early):
            split_tile(
                raw[ker, :, lag, :], ker, slice(lag * width, (lag + 1) * width), halves
            )


def first_block_kernel(prestress_ref, friction_ref, load_ref, out_ref):
    patch_count, width = prestress_ref.shape
    times = times_of(0, width)
    for patch in range(patch_count):
        row = pl.ds(patch, 1)
        drive = prestress_ref[row, :] + load_ref[row, :] * times
        out_ref[patch] = friction_solve(drive, jnp.broadcast_to(friction_ref[row, :], drive.shape))


def product(left, halves, parts):
    right = jnp.concatenate([halves[part] for part in parts], axis=1)
    return jnp.dot(left, right, preferred_element_type=jnp.float32)


def convolve_and_route(
    window, stacked, responses, sums, early, late, table_ref, keep_ref, send_ref, late_ready=None
):
    slots, span, width = window.shape
    history = span - BLOCK
    ker_count = responses.shape[0]
    early_lags, late_lags = early.shape[1] // width, late.shape[1] // width
    chunk = stacked.shape[0] // (2 * BLOCK)
    rows = chunk * BLOCK
    chunks = slots // chunk
    if late_ready is not None and chunks > 1:
        late_ready()

    def one_chunk(chunk_idx, carry):
        first = chunk_idx * chunk

        def part(halves, lags):
            for lag in lags:
                cols = slice(lag * width, (lag + 1) * width)
                for slot in range(chunk):
                    upper, lower = split(
                        window[first + slot, history - lag : history - lag + BLOCK, :]
                    )
                    stacked[slot * BLOCK : (slot + 1) * BLOCK, cols] = upper
                    stacked[rows + slot * BLOCK : rows + (slot + 1) * BLOCK, cols] = lower
            taps = slice(lags[0] * width, (lags[-1] + 1) * width)
            both = product(stacked[:, taps], halves, range(ker_count))
            rest = product(stacked[:rows, taps], halves, range(ker_count, 2 * ker_count))
            return both[:rows] + both[rows:] + rest

        total = part(early, range(early_lags))
        if late_ready is not None and chunks == 1:
            late_ready()
        total = total + part(late, range(early_lags, early_lags + late_lags))
        for ker in range(ker_count):
            for slot in range(chunk):
                responses[ker, first + slot, history:, :] = total[
                    slot * BLOCK : (slot + 1) * BLOCK, ker * width : (ker + 1) * width
                ]
        return carry

    if chunks == 1:
        one_chunk(0, 0)
    else:
        lax.fori_loop(0, chunks, one_chunk, 0)

    per_kernel = table_ref.shape[1] // ker_count
    for ker in range(ker_count):
        sums[ker][...] = jnp.zeros_like(sums[ker])
    for entry in range(per_kernel):
        for ker in range(ker_count):
            idx = ker * per_kernel + entry
            place = table_ref[0, idx]
            sums[ker][place] = (
                sums[ker][place]
                + responses[ker, table_ref[1, idx], pl.ds(table_ref[2, idx], BLOCK), :]
            )
    half = keep_ref.shape[0]
    for place in range(2 * half):
        total = sums[0][place]
        for ker in range(1, ker_count):
            total = total + sums[ker][place]
        if place < half:
            keep_ref[place] = total
        else:
            send_ref[place - half] = total


def first_stress_kernel(
    table_ref, wanted_ref, params_ref, early, kernel_ref,
    keep_ref, send_ref, rates_tail_ref, responses_tail_ref, late,
    window, stacked, responses, raw, sem, *sums,
):
    slots, span, width = window.shape
    loaded = raw.shape[2]
    lag_count = kernel_ref.shape[2]
    load = pltpu.make_async_copy(
        kernel_ref.at[:, :, lag_count - loaded :, :], raw, sem
    )
    load.start()

    def late_ready():
        load.wait()
        late_lags = late.shape[1] // width
        for lag in range(late_lags):
            split_lag(lag, raw, loaded - late_lags, late)

    history = span - BLOCK
    patch_count = (params_ref.shape[1] - 1) // 3
    times = times_of(0, width)
    for ker in range(responses.shape[0]):
        responses[ker, :, :history, :] = jnp.zeros((slots, history, width), jnp.float32)

    patches = lax.broadcasted_iota(jnp.int32, (patch_count, width), 0).astype(jnp.float32)

    def one_slot(slot):
        chosen = patches == wanted_ref[pl.ds(slot, 1), :]

        def field(number):
            rows = params_ref[slot, number * patch_count : (number + 1) * patch_count, :]
            return jnp.sum(jnp.where(chosen, rows, 0.0), axis=0, keepdims=True)

        drive = field(0) + field(2) * times
        friction = jnp.broadcast_to(field(1), drive.shape)
        window[slot, :history, :] = jnp.zeros((history, width), jnp.float32)
        window[slot, history:, :] = friction_solve(drive, friction)

    if slots <= 8:
        for slot in range(slots):
            one_slot(slot)
    else:
        pl.loop(0, slots)(one_slot)
    convolve_and_route(
        window, stacked, responses, sums, early, late, table_ref, keep_ref, send_ref, late_ready
    )
    rates_tail_ref[...] = window[:, BLOCK:, :]
    responses_tail_ref[...] = responses[:, :, BLOCK:, :]


def next_stress_kernel(
    table_ref, rates_ref, rates_tail_ref, responses_tail_ref, early, late,
    keep_ref, send_ref,
    window, stacked, responses, *sums,
):
    history = window.shape[1] - BLOCK
    window[:, :history, :] = rates_tail_ref[...]
    window[:, history:, :] = rates_ref[...]
    responses[:, :, :history, :] = responses_tail_ref[...]
    convolve_and_route(
        window, stacked, responses, sums, early, late, table_ref, keep_ref, send_ref
    )


def solve_patch(block_idx, patch, prestress_ref, friction_ref, load_ref, kept_ref, came_ref):
    width = prestress_ref.shape[1]
    row = pl.ds(patch, 1)
    stress = kept_ref[patch] + came_ref[patch]
    drive = prestress_ref[row, :] + load_ref[row, :] * times_of(block_idx, width) + stress
    return friction_solve(drive, jnp.broadcast_to(friction_ref[row, :], drive.shape))


def middle_block_kernel(
    asked_ref, prestress_ref, friction_ref, load_ref, kept_ref, came_ref, rates_ref, outgoing_ref
):
    for patch in range(prestress_ref.shape[0]):
        rates_ref[patch] = solve_patch(
            1, patch, prestress_ref, friction_ref, load_ref, kept_ref, came_ref
        )

    def one_slot(slot):
        outgoing_ref[slot] = rates_ref[asked_ref[slot]]

    slots = outgoing_ref.shape[0]
    if slots <= 8:
        for slot in range(slots):
            one_slot(slot)
    else:
        pl.loop(0, slots)(one_slot)


def last_block_kernel(
    prestress_ref, friction_ref, load_ref, kept_ref, came_ref, first_ref, second_ref, out_ref
):
    for patch in range(prestress_ref.shape[0]):
        out_ref[patch, :BLOCK, :] = first_ref[patch]
        out_ref[patch, BLOCK : 2 * BLOCK, :] = second_ref[patch]
        out_ref[patch, 2 * BLOCK :, :] = solve_patch(
            2, patch, prestress_ref, friction_ref, load_ref, kept_ref, came_ref
        )


def local(interactions, list_lengths, kernels, prestress, friction, load_rate):
    n_recv = lax.axis_size("recv")
    n_src = lax.axis_size("src")
    ker_count, width, lag_count, _ = kernels.shape
    patch_count = prestress.shape[0]
    group_rows = n_src * patch_count
    bits = n_src.bit_length() - 1
    assert n_src == 1 << bits and bits > 0

    f32, bf16 = jnp.float32, jnp.bfloat16
    packed = pl.pallas_call(
        pack_kernel,
        in_specs=[VMEM] * 4,
        out_specs=VMEM,
        out_shape=jax.ShapeDtypeStruct((n_recv, 3 * patch_count + 1, width), f32),
        name="pack",
    )(interactions, prestress, friction, load_rate)
    received = lax.all_to_all(packed, "recv", split_axis=0, concat_axis=0, tiled=True)
    asked = received[:, -1, 0].astype(jnp.int32)

    late_lags = lag_count // 4
    early = jax.ShapeDtypeStruct((2 * ker_count, (lag_count - late_lags) * width, width), bf16)
    late = jax.ShapeDtypeStruct((2 * ker_count, late_lags * width, width), bf16)
    kernels = pltpu.with_memory_space_constraint(kernels, pltpu.HBM)
    early, table, wanted = pl.pallas_call(
        functools.partial(prepare_kernel, patch_count),
        in_specs=[SMEM, HBM, HBM],
        out_specs=[VMEM] * 3,
        out_shape=[
            early,
            jax.ShapeDtypeStruct(interactions.shape, jnp.int32),
            jax.ShapeDtypeStruct((n_recv, width), f32),
        ],
        scratch_shapes=[
            pltpu.VMEM(interactions.shape, jnp.int32),
            pltpu.VMEM(kernels.shape, f32),
            pltpu.SemaphoreType.DMA,
            pltpu.SemaphoreType.DMA((ker_count,)),
        ],
        compiler_params=grant(12),
        name="prepare",
    )(list_lengths, pltpu.with_memory_space_constraint(interactions, pltpu.HBM), kernels)
    first_rates = pl.pallas_call(
        first_block_kernel,
        in_specs=[VMEM] * 3,
        out_specs=VMEM,
        out_shape=jax.ShapeDtypeStruct((patch_count, BLOCK, width), f32),
        compiler_params=grant(2),
        name="first_block",
    )(prestress, friction, load_rate)

    half = jax.ShapeDtypeStruct((group_rows // 2, BLOCK, width), f32)
    rates_tail = jax.ShapeDtypeStruct((n_recv, lag_count, width), f32)
    responses_tail = jax.ShapeDtypeStruct((ker_count, n_recv, lag_count, width), f32)
    chunk = min(8, n_recv)
    stress_mib = 16 + 8 * ker_count * n_recv * (lag_count + BLOCK) * width // 2**20
    scratch = [
        pltpu.VMEM((n_recv, lag_count + BLOCK, width), f32),
        pltpu.VMEM((2 * chunk * BLOCK, lag_count * width), bf16),
        pltpu.VMEM((ker_count, n_recv, lag_count + BLOCK, width), f32),
    ] + [pltpu.VMEM((group_rows + 1, BLOCK, width), f32)] * ker_count

    def reduce_scatter(kept, sent):
        for bit in range(bits):
            pairs = [(i, i ^ (1 << bit)) for i in range(n_src)]
            came = lax.ppermute(sent, "src", pairs)
            if bit == bits - 1:
                return kept, came
            quarter = kept.shape[0] // 2
            sent = kept[quarter:] + came[quarter:]
            kept = kept[:quarter] + came[:quarter]

    loaded = min(lag_count, -(-late_lags // 8) * 8)
    kept, sent, rates_tail, responses_tail, late = pl.pallas_call(
        first_stress_kernel,
        in_specs=[SMEM] + [VMEM] * 3 + [HBM],
        out_specs=[VMEM] * 5,
        out_shape=[half, half, rates_tail, responses_tail, late],
        scratch_shapes=scratch[:3]
        + [pltpu.VMEM((ker_count, width, loaded, width), f32), pltpu.SemaphoreType.DMA]
        + scratch[3:],
        compiler_params=grant(stress_mib),
        name="first_stress",
    )(table, wanted, received, early, kernels)
    kept, came = reduce_scatter(kept, sent)
    second_rates, outgoing = pl.pallas_call(
        middle_block_kernel,
        in_specs=[SMEM] + [VMEM] * 5,
        out_specs=[VMEM] * 2,
        out_shape=[
            jax.ShapeDtypeStruct((patch_count, BLOCK, width), f32),
            jax.ShapeDtypeStruct((n_recv, BLOCK, width), f32),
        ],
        compiler_params=grant(4),
        name="middle_block",
    )(asked, prestress, friction, load_rate, kept, came)
    rates = lax.all_to_all(outgoing, "recv", split_axis=0, concat_axis=0, tiled=True)
    kept, sent = pl.pallas_call(
        next_stress_kernel,
        in_specs=[SMEM] + [VMEM] * 5,
        out_specs=[VMEM] * 2,
        out_shape=[half, half],
        scratch_shapes=scratch,
        compiler_params=grant(stress_mib),
        name="next_stress",
    )(table, rates, rates_tail, responses_tail, early, late)
    kept, came = reduce_scatter(kept, sent)
    return pl.pallas_call(
        last_block_kernel,
        in_specs=[VMEM] * 7,
        out_specs=VMEM,
        out_shape=jax.ShapeDtypeStruct((patch_count, BLOCKS * BLOCK, width), f32),
        compiler_params=grant(4),
        name="last_block",
    )(prestress, friction, load_rate, kept, came, first_rates, second_rates)


def solution(mesh):
    in_specs = (
        P(None, ("recv", "src")),
        P(("recv", "src")),
        P(("recv", "src"), None, None, None),
        P(("recv", "src"), None),
        P(("recv", "src"), None),
        P(("recv", "src"), None),
    )
    out_specs = P(("recv", "src"), None, None)
    return jax.shard_map(local, mesh=mesh, in_specs=in_specs, out_specs=out_specs, check_vma=False)
```

```python
import functools

import jax
import jax.numpy as jnp
from jax import lax
from jax.experimental import pallas as pl
from jax.experimental.pallas import tpu as pltpu
from jax.sharding import PartitionSpec as P

BLOCK = 32
BLOCKS = 3
NEWTON = 4
PAD = 8
damping = 0.5
def grant(mib):
    return pltpu.CompilerParams(vmem_limit_bytes=mib * 2**20)


VMEM = pl.BlockSpec(memory_space=pltpu.VMEM)
SMEM = pl.BlockSpec(memory_space=pltpu.SMEM)
HBM = pl.BlockSpec(memory_space=pltpu.HBM)


def in_hbm(array):
    return pltpu.with_memory_space_constraint(array, pltpu.HBM)


def friction_solve(drive, friction):
    rates = drive / (damping + friction)
    for newton_step in range(NEWTON - 1):
        squares = 1.0 + rates * rates
        inverse_root = lax.rsqrt(squares)
        magnitude = jnp.log(jnp.abs(rates) + squares * inverse_root)
        inverse_sinh = jnp.where(rates < 0, -magnitude, magnitude)
        misfit = damping * rates + friction * inverse_sinh - drive
        rates = rates - misfit / (damping + friction * inverse_root)
    return rates


def times_of(block_idx, width):
    steps = lax.broadcasted_iota(jnp.int32, (BLOCK, width), 0)
    return (steps + (block_idx * BLOCK + 1)).astype(jnp.float32)


def split(values):
    high = values.astype(jnp.bfloat16)
    return high, (values - high.astype(jnp.float32)).astype(jnp.bfloat16)


def wanted_patches(interactions_ref, slots, patch_count):
    sources = interactions_ref[pl.ds(1, 1), :]
    owners = lax.broadcasted_iota(jnp.int32, (slots, sources.shape[1]), 0)
    first = (owners * lax.axis_size("src") + lax.axis_index("src")) * patch_count
    offset = sources - first
    inside = (offset >= 0) & (offset < patch_count)
    wanted = jnp.max(jnp.where(inside, offset, 0).astype(jnp.float32), axis=1, keepdims=True)
    return owners, inside, wanted


def pack_kernel(interactions_ref, prestress_ref, friction_ref, load_ref, out_ref):
    slots, rows, width = out_ref.shape
    patch_count = prestress_ref.shape[0]
    wanted = wanted_patches(interactions_ref, slots, patch_count)[2]
    wanted = jnp.broadcast_to(wanted, (slots, width))
    for field, ref in enumerate((prestress_ref, friction_ref, load_ref)):
        out_ref[:, field * patch_count : (field + 1) * patch_count, :] = jnp.broadcast_to(
            ref[...][None], (slots, patch_count, width)
        )
    for slot in range(slots):
        out_ref[slot, rows - 1 :, :] = wanted[slot : slot + 1, :]


def split_lag(lag, raw, ker, halves, number):
    width = raw.shape[3]
    rows = raw.reshape(raw.shape[0], width * raw.shape[2], width)
    tile = rows[ker, pl.ds(lag, width, stride=raw.shape[2]), :]
    cols = slice(number * width, (number + 1) * width)
    halves[ker, :, cols], halves[halves.shape[0] // 2 + ker, :, cols] = split(tile)


def prepare_kernel(
    patch_count, lengths_ref, interactions_ref, kernel_ref, early, late_ref, table_ref, wanted_ref,
    interactions, lengths, raw, late, list_sems, load_sems, store_sems,
):
    ker_count, _, lag_count, width = kernel_ref.shape
    early_lags = early.shape[2] // width
    loads = [
        pltpu.make_async_copy(kernel_ref.at[ker], raw.at[ker, :, :lag_count, :], load_sems.at[ker])
        for ker in range(ker_count)
    ]
    list_loads = [
        pltpu.make_async_copy(interactions_ref, interactions, list_sems.at[0]),
        pltpu.make_async_copy(lengths_ref, lengths, list_sems.at[1]),
    ]
    for copy in list_loads + loads:
        copy.start()
    for copy in list_loads:
        copy.wait()

    slots = wanted_ref.shape[0]
    owners, inside, wanted = wanted_patches(interactions, slots, patch_count)
    wanted_ref[...] = jnp.broadcast_to(wanted, wanted_ref.shape)
    n_src = lax.axis_size("src")
    group_rows = n_src * patch_count
    receivers = interactions[pl.ds(0, 1), :] - lax.axis_index("recv") * group_rows
    strips = jnp.zeros_like(receivers)
    for other in range(1, n_src):
        strips = strips + (receivers >= other * patch_count).astype(jnp.int32)
    distance = strips ^ lax.axis_index("src")
    bits = n_src.bit_length() - 1
    order = jnp.zeros_like(distance)
    for bit in range(bits):
        order = order | (((distance >> bit) & 1) << (bits - 1 - bit))
    place = order * patch_count + receivers - strips * patch_count
    entry_numbers = lax.broadcasted_iota(jnp.int32, place.shape, 1)
    place = jnp.where(entry_numbers < lengths[0], place, group_rows)
    table_ref[pl.ds(0, 1), :] = place * BLOCK
    owner = jnp.max(
        jnp.where(inside, owners, 0).astype(jnp.float32), axis=0, keepdims=True
    ).astype(jnp.int32)
    ker_of = jnp.zeros_like(place)
    per_kernel = place.shape[1] // ker_count
    for ker in range(1, ker_count):
        ker_of = ker_of + (entry_numbers >= ker * per_kernel).astype(jnp.int32)
    span = lag_count + BLOCK
    table_ref[pl.ds(1, 1), :] = (
        (ker_of * slots + owner) * span + span - interactions[pl.ds(2, 1), :]
    )

    stores = [
        pltpu.make_async_copy(late.at[part], late_ref.at[part], store_sems.at[part])
        for part in range(2 * ker_count)
    ]
    for ker in range(ker_count):
        loads[ker].wait()
        for lag in range(early_lags, lag_count):
            split_lag(lag, raw, ker, late, lag - early_lags)
        stores[ker].start()
        stores[ker_count + ker].start()
        for lag in range(early_lags):
            split_lag(lag, raw, ker, early, lag)
    for copy in stores:
        copy.wait()


def first_block_kernel(prestress_ref, friction_ref, load_ref, out_ref):
    patch_count, width = prestress_ref.shape
    times = times_of(0, width)
    for patch in range(patch_count):
        row = pl.ds(patch, 1)
        drive = prestress_ref[row, :] + load_ref[row, :] * times
        out_ref[patch] = friction_solve(drive, jnp.broadcast_to(friction_ref[row, :], drive.shape))


def product(left, halves, parts):
    right = jnp.concatenate([halves[part] for part in parts], axis=0)
    return lax.dot_general(
        left, right, (((1,), (1,)), ((), ())), preferred_element_type=jnp.float32
    )


def convolve_and_route(
    window, stacked, responses, sums, early, late, late_copy, table_ref, totals
):
    slots, span, width = window.shape
    history = span - BLOCK
    ker_count = responses.shape[0]
    early_lags, late_lags = early.shape[2] // width, late.shape[2] // width
    chunk = stacked.shape[0] // (2 * BLOCK)
    rows = chunk * BLOCK
    chunks = slots // chunk

    def clear():
        for ker in range(ker_count):
            sums[ker][...] = jnp.zeros_like(sums[ker])

    if chunks > 1:
        clear()
        if late_copy is not None:
            late_copy.wait()

    def one_chunk(chunk_idx, carry):
        first = chunk_idx * chunk

        for lag in range(early_lags + late_lags):
            cols = slice(lag * width, (lag + 1) * width)
            for slot in range(chunk):
                upper, lower = split(
                    window[first + slot, history - lag : history - lag + BLOCK, :]
                )
                stacked[slot * BLOCK : (slot + 1) * BLOCK, cols] = upper
                stacked[rows + slot * BLOCK : rows + (slot + 1) * BLOCK, cols] = lower
        if chunks == 1:
            clear()

        def part(halves, taps):
            both = product(stacked[:, taps], halves, range(ker_count))
            rest = product(stacked[:rows, taps], halves, range(ker_count, 2 * ker_count))
            return both[:rows] + both[rows:] + rest

        total = part(early, slice(0, early_lags * width))
        if chunks == 1 and late_copy is not None:
            late_copy.wait()
        total = total + part(late, slice(early_lags * width, (early_lags + late_lags) * width))
        for ker in range(ker_count):
            for slot in range(chunk):
                responses[ker, first + slot, history:, :] = total[
                    slot * BLOCK : (slot + 1) * BLOCK, ker * width : (ker + 1) * width
                ]
        return carry

    if chunks == 1:
        one_chunk(0, 0)
    else:
        lax.fori_loop(0, chunks, one_chunk, 0)

    per_kernel = table_ref.shape[1] // ker_count
    every = responses.reshape(ker_count * slots * span, width)
    for entry in range(per_kernel):
        for ker in range(ker_count):
            idx = ker * per_kernel + entry
            place = pl.ds(pl.multiple_of(table_ref[0, idx], BLOCK), BLOCK)
            sums[ker][place, :] = sums[ker][place, :] + every[pl.ds(table_ref[1, idx], BLOCK), :]
    strips = totals[0].shape[0]
    patches = totals[0].shape[1]
    for group in range(2):
        for place in range(2 * strips * patches):
            part, strip, patch = place // (strips * patches), place // patches % strips, place % patches
            first = (part * strips + strip) * 2 * patches + group * patches + patch
            rows = slice(first * BLOCK, (first + 1) * BLOCK)
            total = sums[0][rows, :]
            for ker in range(1, ker_count):
                total = total + sums[ker][rows, :]
            totals[2 * group + part][strip, patch] = total


def first_stress_kernel(
    table_ref, wanted_ref, params_ref, early, late_ref,
    *refs,
):
    totals, (rates_tail_ref, responses_tail_ref, late) = refs[:4], refs[4:7]
    window, stacked, responses, late_sem, *sums = refs[7:]
    late_copy = pltpu.make_async_copy(late_ref.at[: late.shape[0]], late, late_sem)
    late_copy.start()
    slots, span, width = window.shape
    history = span - BLOCK
    patch_count = (params_ref.shape[1] - 1) // 3
    times = times_of(0, width)
    for ker in range(responses.shape[0]):
        responses[ker, :, :history, :] = jnp.zeros((slots, history, width), jnp.float32)

    patches = lax.broadcasted_iota(jnp.int32, (patch_count, width), 0).astype(jnp.float32)

    def one_slot(slot):
        chosen = patches == wanted_ref[pl.ds(slot, 1), :]

        def field(number):
            rows = params_ref[slot, number * patch_count : (number + 1) * patch_count, :]
            return jnp.sum(jnp.where(chosen, rows, 0.0), axis=0, keepdims=True)

        drive = field(0) + field(2) * times
        friction = jnp.broadcast_to(field(1), drive.shape)
        window[slot, :history, :] = jnp.zeros((history, width), jnp.float32)
        window[slot, history:, :] = friction_solve(drive, friction)

    if slots <= 8:
        for slot in range(slots):
            one_slot(slot)
    else:
        pl.loop(0, slots)(one_slot)
    convolve_and_route(
        window, stacked, responses, sums, early, late, late_copy, table_ref, totals
    )
    rates_tail_ref[...] = window[:, BLOCK:, :]
    responses_tail_ref[...] = responses[:, :, BLOCK:, :]


def next_stress_kernel(
    table_ref, rates_ref, rates_tail_ref, responses_tail_ref, early, late,
    *refs,
):
    totals, (window, stacked, responses, *sums) = refs[:4], refs[4:]
    history = window.shape[1] - BLOCK
    window[:, :history, :] = rates_tail_ref[...]
    window[:, history:, :] = rates_ref[...]
    responses[:, :, :history, :] = responses_tail_ref[...]
    convolve_and_route(
        window, stacked, responses, sums, early, late, None, table_ref, totals
    )


def solve_patch(
    block_idx, patch, first, prestress_ref, friction_ref, load_ref, kept_ref, came_ref
):
    width = prestress_ref.shape[1]
    row = pl.ds(first + patch, 1)
    stress = kept_ref[0, patch] + came_ref[0, patch]
    drive = prestress_ref[row, :] + load_ref[row, :] * times_of(block_idx, width) + stress
    return friction_solve(drive, jnp.broadcast_to(friction_ref[row, :], drive.shape))


def solve_group_kernel(
    block_idx, group, prestress_ref, friction_ref, load_ref, kept_ref, came_ref, rates_ref
):
    patches = rates_ref.shape[0]
    for patch in range(patches):
        rates_ref[patch] = solve_patch(
            block_idx, patch, group * patches, prestress_ref, friction_ref, load_ref,
            kept_ref, came_ref,
        )


def middle_block_kernel(
    asked_ref, prestress_ref, friction_ref, load_ref, kept_ref, came_ref, others_ref,
    rates_ref, outgoing_ref,
):
    patches = others_ref.shape[0]
    for patch in range(patches):
        rates_ref[patch] = others_ref[patch]
        rates_ref[patches + patch] = solve_patch(
            1, patch, patches, prestress_ref, friction_ref, load_ref, kept_ref, came_ref
        )

    def one_slot(slot):
        outgoing_ref[slot] = rates_ref[asked_ref[slot]]

    slots = outgoing_ref.shape[0]
    if slots <= 8:
        for slot in range(slots):
            one_slot(slot)
    else:
        pl.loop(0, slots)(one_slot)


def last_block_kernel(
    prestress_ref, friction_ref, load_ref, kept_ref, came_ref, others_ref, first_ref, second_ref,
    out_ref,
):
    patches = others_ref.shape[0]
    for patch in range(2 * patches):
        out_ref[patch, :BLOCK, :] = first_ref[patch]
        out_ref[patch, BLOCK : 2 * BLOCK, :] = second_ref[patch]
    for patch in range(patches):
        out_ref[patch, 2 * BLOCK :, :] = others_ref[patch]
        out_ref[patches + patch, 2 * BLOCK :, :] = solve_patch(
            2, patch, patches, prestress_ref, friction_ref, load_ref, kept_ref, came_ref
        )


def local(interactions, list_lengths, kernels, prestress, friction, load_rate):
    n_recv = lax.axis_size("recv")
    n_src = lax.axis_size("src")
    ker_count, width, lag_count, _ = kernels.shape
    patch_count = prestress.shape[0]
    group_rows = n_src * patch_count
    bits = n_src.bit_length() - 1
    assert n_src == 1 << bits and bits > 0

    f32, bf16 = jnp.float32, jnp.bfloat16
    packed = pl.pallas_call(
        pack_kernel,
        in_specs=[VMEM] * 4,
        out_specs=VMEM,
        out_shape=jax.ShapeDtypeStruct((n_recv, 3 * patch_count + 1, width), f32),
        compiler_params=grant(2 + n_recv // 8),
        name="pack",
    )(*map(in_hbm, (interactions, prestress, friction, load_rate)))
    received = lax.all_to_all(packed, "recv", split_axis=0, concat_axis=0, tiled=True)
    asked = received[:, -1, 0].astype(jnp.int32)

    late_lags = lag_count // 4
    early = jax.ShapeDtypeStruct((2 * ker_count, width, (lag_count - late_lags) * width), bf16)
    late_shape = (2 * ker_count, width, late_lags * width)
    late_halves = pltpu.VMEM(late_shape, bf16)
    kernels = in_hbm(kernels)
    early, late, table, wanted = pl.pallas_call(
        functools.partial(prepare_kernel, patch_count),
        in_specs=[HBM] * 3,
        out_specs=[VMEM, HBM, VMEM, VMEM],
        out_shape=[
            early,
            jax.ShapeDtypeStruct((24 * ker_count,) + late_shape[1:], bf16),
            jax.ShapeDtypeStruct((2, interactions.shape[1]), jnp.int32),
            jax.ShapeDtypeStruct((n_recv, width), f32),
        ],
        scratch_shapes=[
            pltpu.VMEM(interactions.shape, jnp.int32),
            pltpu.SMEM(list_lengths.shape, jnp.int32),
            pltpu.VMEM((ker_count, width, lag_count + PAD, width), f32),
            late_halves,
            pltpu.SemaphoreType.DMA((2,)),
            pltpu.SemaphoreType.DMA((ker_count,)),
            pltpu.SemaphoreType.DMA((2 * ker_count,)),
        ],
        compiler_params=grant(46),
        name="prepare",
    )(list_lengths, in_hbm(interactions), kernels)
    late_shape, late = jax.ShapeDtypeStruct(late_shape, bf16), in_hbm(late)
    first_rates = pl.pallas_call(
        first_block_kernel,
        in_specs=[VMEM] * 3,
        out_specs=VMEM,
        out_shape=jax.ShapeDtypeStruct((patch_count, BLOCK, width), f32),
        compiler_params=grant(2),
        name="first_block",
    )(prestress, friction, load_rate)

    group_patches = patch_count // 2
    half = jax.ShapeDtypeStruct((n_src // 2, group_patches, BLOCK, width), f32)
    rates_tail = jax.ShapeDtypeStruct((n_recv, lag_count, width), f32)
    responses_tail = jax.ShapeDtypeStruct((ker_count, n_recv, lag_count, width), f32)
    chunk = min(8, n_recv)
    stress_mib = 16 + 8 * ker_count * n_recv * (lag_count + BLOCK) * width // 2**20
    scratch = [
        pltpu.VMEM((n_recv, lag_count + BLOCK, width), f32),
        pltpu.VMEM((2 * chunk * BLOCK, lag_count * width), bf16),
        pltpu.VMEM((ker_count, n_recv, lag_count + BLOCK, width), f32),
    ] + [pltpu.VMEM(((group_rows + 1) * BLOCK, width), f32)] * ker_count

    def reduce_scatter(kept, sent):
        for bit in range(bits):
            pairs = [(i, i ^ (1 << bit)) for i in range(n_src)]
            came = lax.ppermute(sent, "src", pairs)
            if bit == bits - 1:
                return kept, came
            quarter = kept.shape[0] // 2
            sent = kept[quarter:] + came[quarter:]
            kept = kept[:quarter] + came[:quarter]

    rates_group = jax.ShapeDtypeStruct((group_patches, BLOCK, width), f32)

    def solve_first_group(block_idx, terms):
        return pl.pallas_call(
            functools.partial(solve_group_kernel, block_idx, 0),
            in_specs=[VMEM] * 5,
            out_specs=VMEM,
            out_shape=rates_group,
            compiler_params=grant(2),
            name="solve_group",
        )(prestress, friction, load_rate, *terms)

    *totals, rates_tail, responses_tail, late = pl.pallas_call(
        first_stress_kernel,
        in_specs=[SMEM] + [VMEM] * 3 + [HBM],
        out_specs=[VMEM] * 7,
        out_shape=[half] * 4 + [rates_tail, responses_tail, late_shape],
        scratch_shapes=scratch[:3] + [pltpu.SemaphoreType.DMA] + scratch[3:],
        compiler_params=grant(stress_mib),
        name="first_stress",
    )(table, wanted, received, early, late)
    terms = [reduce_scatter(*totals[:2]), reduce_scatter(*totals[2:])]
    second_rates, outgoing = pl.pallas_call(
        middle_block_kernel,
        in_specs=[SMEM] + [VMEM] * 6,
        out_specs=[VMEM] * 2,
        out_shape=[
            jax.ShapeDtypeStruct((patch_count, BLOCK, width), f32),
            jax.ShapeDtypeStruct((n_recv, BLOCK, width), f32),
        ],
        compiler_params=grant(4),
        name="middle_block",
    )(asked, prestress, friction, load_rate, *terms[1], solve_first_group(1, terms[0]))
    rates = lax.all_to_all(outgoing, "recv", split_axis=0, concat_axis=0, tiled=True)
    totals = pl.pallas_call(
        next_stress_kernel,
        in_specs=[SMEM] + [VMEM] * 5,
        out_specs=[VMEM] * 4,
        out_shape=[half] * 4,
        scratch_shapes=scratch,
        compiler_params=grant(stress_mib),
        name="next_stress",
    )(table, rates, rates_tail, responses_tail, early, late)
    terms = [reduce_scatter(*totals[:2]), reduce_scatter(*totals[2:])]
    return pl.pallas_call(
        last_block_kernel,
        in_specs=[VMEM] * 8,
        out_specs=VMEM,
        out_shape=jax.ShapeDtypeStruct((patch_count, BLOCKS * BLOCK, width), f32),
        compiler_params=grant(4),
        name="last_block",
    )(
        prestress, friction, load_rate, *terms[1], solve_first_group(2, terms[0]),
        first_rates, second_rates,
    )


def solution(mesh):
    in_specs = (
        P(None, ("recv", "src")),
        P(("recv", "src")),
        P(("recv", "src"), None, None, None),
        P(("recv", "src"), None),
        P(("recv", "src"), None),
        P(("recv", "src"), None),
    )
    out_specs = P(("recv", "src"), None, None)
    return jax.shard_map(local, mesh=mesh, in_specs=in_specs, out_specs=out_specs, check_vma=False)
```

```python
import functools

import jax
import jax.numpy as jnp
from jax import lax
from jax.experimental import pallas as pl
from jax.experimental.pallas import tpu as pltpu
from jax.sharding import PartitionSpec as P

BLOCK = 32
BLOCKS = 3
NEWTON = 4
PAD = 8
damping = 0.5
def grant(mib):
    return pltpu.CompilerParams(vmem_limit_bytes=mib * 2**20)


VMEM = pl.BlockSpec(memory_space=pltpu.VMEM)
SMEM = pl.BlockSpec(memory_space=pltpu.SMEM)
HBM = pl.BlockSpec(memory_space=pltpu.HBM)


def in_hbm(array):
    return pltpu.with_memory_space_constraint(array, pltpu.HBM)


def friction_solve(drive, friction):
    rates = drive / (damping + friction)
    for newton_step in range(NEWTON - 1):
        squares = 1.0 + rates * rates
        inverse_root = lax.rsqrt(squares)
        magnitude = jnp.log(jnp.abs(rates) + squares * inverse_root)
        inverse_sinh = jnp.where(rates < 0, -magnitude, magnitude)
        misfit = damping * rates + friction * inverse_sinh - drive
        rates = rates - misfit / (damping + friction * inverse_root)
    return rates


def times_of(block_idx, width):
    steps = lax.broadcasted_iota(jnp.int32, (BLOCK, width), 0)
    return (steps + (block_idx * BLOCK + 1)).astype(jnp.float32)


def split(values):
    high = values.astype(jnp.bfloat16)
    return high, (values - high.astype(jnp.float32)).astype(jnp.bfloat16)


def wanted_patches(interactions_ref, slots, patch_count):
    sources = interactions_ref[pl.ds(1, 1), :]
    owners = lax.broadcasted_iota(jnp.int32, (slots, sources.shape[1]), 0)
    first = (owners * lax.axis_size("src") + lax.axis_index("src")) * patch_count
    offset = sources - first
    inside = (offset >= 0) & (offset < patch_count)
    wanted = jnp.max(jnp.where(inside, offset, 0).astype(jnp.float32), axis=1, keepdims=True)
    return owners, inside, wanted


def pack_kernel(interactions_ref, prestress_ref, friction_ref, load_ref, out_ref):
    slots, rows, width = out_ref.shape
    patch_count = prestress_ref.shape[0]
    wanted = wanted_patches(interactions_ref, slots, patch_count)[2]
    wanted = jnp.broadcast_to(wanted, (slots, width))
    for field, ref in enumerate((prestress_ref, friction_ref, load_ref)):
        out_ref[:, field * patch_count : (field + 1) * patch_count, :] = jnp.broadcast_to(
            ref[...][None], (slots, patch_count, width)
        )
    for slot in range(slots):
        out_ref[slot, rows - 1 :, :] = wanted[slot : slot + 1, :]


def split_lag(lag, raw, ker, halves, number):
    width = raw.shape[3]
    rows = raw.reshape(raw.shape[0], width * raw.shape[2], width)
    tile = rows[ker, pl.ds(lag, width, stride=raw.shape[2]), :]
    cols = slice(number * width, (number + 1) * width)
    halves[ker, :, cols], halves[halves.shape[0] // 2 + ker, :, cols] = split(tile)


def prepare_kernel(
    patch_count, lengths_ref, interactions_ref, kernel_ref, early, late_ref, table_ref, wanted_ref,
    interactions, lengths, raw, late, list_sems, load_sems, store_sems,
):
    ker_count, _, lag_count, width = kernel_ref.shape
    early_lags = early.shape[2] // width
    loads = [
        pltpu.make_async_copy(kernel_ref.at[ker], raw.at[ker, :, :lag_count, :], load_sems.at[ker])
        for ker in range(ker_count)
    ]
    list_loads = [
        pltpu.make_async_copy(interactions_ref, interactions, list_sems.at[0]),
        pltpu.make_async_copy(lengths_ref, lengths, list_sems.at[1]),
    ]
    for copy in list_loads + loads:
        copy.start()
    for copy in list_loads:
        copy.wait()

    slots = wanted_ref.shape[0]
    owners, inside, wanted = wanted_patches(interactions, slots, patch_count)
    wanted_ref[...] = jnp.broadcast_to(wanted, wanted_ref.shape)
    n_src = lax.axis_size("src")
    group_rows = n_src * patch_count
    receivers = interactions[pl.ds(0, 1), :] - lax.axis_index("recv") * group_rows
    strips = jnp.zeros_like(receivers)
    for other in range(1, n_src):
        strips = strips + (receivers >= other * patch_count).astype(jnp.int32)
    distance = strips ^ lax.axis_index("src")
    bits = n_src.bit_length() - 1
    order = jnp.zeros_like(distance)
    for bit in range(bits):
        order = order | (((distance >> bit) & 1) << (bits - 1 - bit))
    place = order * patch_count + receivers - strips * patch_count
    entry_numbers = lax.broadcasted_iota(jnp.int32, place.shape, 1)
    place = jnp.where(entry_numbers < lengths[0], place, group_rows)
    table_ref[pl.ds(0, 1), :] = place * BLOCK
    owner = jnp.max(
        jnp.where(inside, owners, 0).astype(jnp.float32), axis=0, keepdims=True
    ).astype(jnp.int32)
    ker_of = jnp.zeros_like(place)
    per_kernel = place.shape[1] // ker_count
    for ker in range(1, ker_count):
        ker_of = ker_of + (entry_numbers >= ker * per_kernel).astype(jnp.int32)
    span = lag_count + BLOCK
    table_ref[pl.ds(1, 1), :] = (
        (ker_of * slots + owner) * span + span - interactions[pl.ds(2, 1), :]
    )

    stores = [
        pltpu.make_async_copy(late.at[part], late_ref.at[part], store_sems.at[part])
        for part in range(2 * ker_count)
    ]
    for ker in range(ker_count):
        loads[ker].wait()
        for lag in range(early_lags, lag_count):
            split_lag(lag, raw, ker, late, lag - early_lags)
        stores[ker].start()
        stores[ker_count + ker].start()
        for lag in range(early_lags):
            split_lag(lag, raw, ker, early, lag)
    for copy in stores:
        copy.wait()


def first_blocks_kernel(
    prestress_ref, friction_ref, load_ref, second_ref, out_ref, rates, sems
):
    patch_count, width = prestress_ref.shape
    second = pltpu.make_async_copy(second_ref, out_ref.at[:, BLOCK : 2 * BLOCK], sems.at[0])
    second.start()
    times = times_of(0, width)
    for patch in range(patch_count):
        row = pl.ds(patch, 1)
        drive = prestress_ref[row, :] + load_ref[row, :] * times
        rates[patch] = friction_solve(drive, jnp.broadcast_to(friction_ref[row, :], drive.shape))
    first = pltpu.make_async_copy(rates, out_ref.at[:, :BLOCK], sems.at[1])
    first.start()
    second.wait()
    first.wait()


def product(left, halves, parts):
    right = jnp.concatenate([halves[part] for part in parts], axis=0)
    return lax.dot_general(
        left, right, (((1,), (1,)), ((), ())), preferred_element_type=jnp.float32
    )


def convolve_and_route(
    window, stacked, responses, sums, early, late, late_copy, table, table_copy, totals
):
    slots, span, width = window.shape
    history = span - BLOCK
    ker_count = responses.shape[0]
    early_lags, late_lags = early.shape[2] // width, late.shape[2] // width
    chunk = stacked.shape[0] // (2 * BLOCK)
    rows = chunk * BLOCK
    chunks = slots // chunk

    def clear():
        for ker in range(ker_count):
            sums[ker][...] = jnp.zeros_like(sums[ker])

    if chunks > 1:
        clear()
        if late_copy is not None:
            late_copy.wait()

    def one_chunk(chunk_idx, carry):
        first = chunk_idx * chunk

        for lag in range(early_lags + late_lags):
            cols = slice(lag * width, (lag + 1) * width)
            for slot in range(chunk):
                upper, lower = split(
                    window[first + slot, history - lag : history - lag + BLOCK, :]
                )
                stacked[slot * BLOCK : (slot + 1) * BLOCK, cols] = upper
                stacked[rows + slot * BLOCK : rows + (slot + 1) * BLOCK, cols] = lower
        if chunks == 1:
            clear()

        def part(halves, taps):
            both = product(stacked[:, taps], halves, range(ker_count))
            rest = product(stacked[:rows, taps], halves, range(ker_count, 2 * ker_count))
            return both[:rows] + both[rows:] + rest

        total = part(early, slice(0, early_lags * width))
        if chunks == 1 and late_copy is not None:
            late_copy.wait()
        total = total + part(late, slice(early_lags * width, (early_lags + late_lags) * width))
        for ker in range(ker_count):
            for slot in range(chunk):
                responses[ker, first + slot, history:, :] = total[
                    slot * BLOCK : (slot + 1) * BLOCK, ker * width : (ker + 1) * width
                ]
        return carry

    if chunks == 1:
        one_chunk(0, 0)
    else:
        lax.fori_loop(0, chunks, one_chunk, 0)

    table_copy.wait()
    per_kernel = table.shape[1] // ker_count
    every = responses.reshape(ker_count * slots * span, width)
    for entry in range(per_kernel):
        for ker in range(ker_count):
            idx = ker * per_kernel + entry
            place = pl.ds(pl.multiple_of(table[0, idx], BLOCK), BLOCK)
            sums[ker][place, :] = sums[ker][place, :] + every[pl.ds(table[1, idx], BLOCK), :]
    strips = totals[0].shape[0]
    counts = totals[0].shape[1], totals[2].shape[1]
    for group in range(2):
        for part in range(2):
            for strip in range(strips):
                for patch in range(counts[group]):
                    place = (part * strips + strip) * sum(counts) + group * counts[0] + patch
                    rows = slice(place * BLOCK, (place + 1) * BLOCK)
                    total = sums[0][rows, :]
                    for ker in range(1, ker_count):
                        total = total + sums[ker][rows, :]
                    totals[2 * group + part][strip, patch] = total


def first_stress_kernel(
    table_ref, wanted_ref, params_ref, early, late_ref,
    *refs,
):
    totals, (rates_tail_ref, responses_tail_ref, late) = refs[:4], refs[4:7]
    window, stacked, responses, late_sem, table, table_sem, *sums = refs[7:]
    table_copy = pltpu.make_async_copy(table_ref, table, table_sem)
    table_copy.start()
    late_copy = pltpu.make_async_copy(late_ref.at[: late.shape[0]], late, late_sem)
    late_copy.start()
    slots, span, width = window.shape
    history = span - BLOCK
    patch_count = (params_ref.shape[1] - 1) // 3
    times = times_of(0, width)
    for ker in range(responses.shape[0]):
        responses[ker, :, :history, :] = jnp.zeros((slots, history, width), jnp.float32)

    patches = lax.broadcasted_iota(jnp.int32, (patch_count, width), 0).astype(jnp.float32)

    def one_slot(slot):
        chosen = patches == wanted_ref[pl.ds(slot, 1), :]

        def field(number):
            rows = params_ref[slot, number * patch_count : (number + 1) * patch_count, :]
            return jnp.sum(jnp.where(chosen, rows, 0.0), axis=0, keepdims=True)

        drive = field(0) + field(2) * times
        friction = jnp.broadcast_to(field(1), drive.shape)
        window[slot, :history, :] = jnp.zeros((history, width), jnp.float32)
        window[slot, history:, :] = friction_solve(drive, friction)

    if slots <= 8:
        for slot in range(slots):
            one_slot(slot)
    else:
        pl.loop(0, slots)(one_slot)
    convolve_and_route(
        window, stacked, responses, sums, early, late, late_copy, table, table_copy, totals
    )
    rates_tail_ref[...] = window[:, BLOCK:, :]
    responses_tail_ref[...] = responses[:, :, BLOCK:, :]


def next_stress_kernel(
    table_ref, rates_ref, rates_tail_ref, responses_tail_ref, early, late,
    *refs,
):
    totals, (window, stacked, responses, table, table_sem, *sums) = refs[:4], refs[4:]
    table_copy = pltpu.make_async_copy(table_ref, table, table_sem)
    table_copy.start()
    history = window.shape[1] - BLOCK
    window[:, :history, :] = rates_tail_ref[...]
    window[:, history:, :] = rates_ref[...]
    responses[:, :, :history, :] = responses_tail_ref[...]
    convolve_and_route(
        window, stacked, responses, sums, early, late, None, table, table_copy, totals
    )


def solve_patch(
    block_idx, patch, first, prestress_ref, friction_ref, load_ref, kept_ref, came_ref
):
    width = prestress_ref.shape[1]
    row = pl.ds(first + patch, 1)
    stress = kept_ref[0, patch] + came_ref[0, patch]
    drive = prestress_ref[row, :] + load_ref[row, :] * times_of(block_idx, width) + stress
    return friction_solve(drive, jnp.broadcast_to(friction_ref[row, :], drive.shape))


def solve_group_kernel(
    block_idx, prestress_ref, friction_ref, load_ref, kept_ref, came_ref, rates_ref
):
    for patch in range(rates_ref.shape[0]):
        rates_ref[patch] = solve_patch(
            block_idx, patch, 0, prestress_ref, friction_ref, load_ref, kept_ref, came_ref
        )


def middle_block_kernel(
    received_ref, prestress_ref, friction_ref, load_ref, kept_ref, came_ref, others_ref,
    rates_ref, outgoing_ref,
):
    known = others_ref.shape[0]
    rates_ref[:known] = others_ref[...]
    for patch in range(rates_ref.shape[0] - known):
        rates_ref[known + patch] = solve_patch(
            1, patch, known, prestress_ref, friction_ref, load_ref, kept_ref, came_ref
        )

    asked_row = received_ref.shape[1] - 1

    def one_slot(slot):
        asked = jnp.broadcast_to(received_ref[slot, asked_row:, :], outgoing_ref.shape[1:])
        chosen = rates_ref[0]
        for patch in range(1, rates_ref.shape[0]):
            chosen = jnp.where(asked == patch, rates_ref[patch], chosen)
        outgoing_ref[slot] = chosen

    slots = outgoing_ref.shape[0]
    if slots <= 8:
        for slot in range(slots):
            one_slot(slot)
    else:
        pl.loop(0, slots)(one_slot)


def last_block_kernel(
    prestress_ref, friction_ref, load_ref, kept_ref, came_ref, others_ref, begun_ref, out_ref,
    rates, sems,
):
    known, patches = others_ref.shape[0], rates.shape[0]
    copies = [
        pltpu.make_async_copy(
            rates.at[patch], out_ref.at[known + patch, 2 * BLOCK :], sems.at[patch]
        )
        for patch in range(patches)
    ]
    others = pltpu.make_async_copy(others_ref, out_ref.at[:known, 2 * BLOCK :], sems.at[patches])
    others.start()
    for patch in range(patches):
        rates[patch] = solve_patch(
            2, patch, known, prestress_ref, friction_ref, load_ref, kept_ref, came_ref
        )
        copies[patch].start()
    for copy in copies + [others]:
        copy.wait()


def local(interactions, list_lengths, kernels, prestress, friction, load_rate):
    n_recv = lax.axis_size("recv")
    n_src = lax.axis_size("src")
    ker_count, width, lag_count, _ = kernels.shape
    patch_count = prestress.shape[0]
    group_rows = n_src * patch_count
    bits = n_src.bit_length() - 1
    assert n_src == 1 << bits and bits > 0

    f32, bf16 = jnp.float32, jnp.bfloat16
    packed = pl.pallas_call(
        pack_kernel,
        in_specs=[VMEM] * 4,
        out_specs=VMEM,
        out_shape=jax.ShapeDtypeStruct((n_recv, 3 * patch_count + 1, width), f32),
        compiler_params=grant(2 + n_recv // 8),
        name="pack",
    )(*map(in_hbm, (interactions, prestress, friction, load_rate)))
    received = lax.all_to_all(packed, "recv", split_axis=0, concat_axis=0, tiled=True)

    late_lags = lag_count // 4
    early = jax.ShapeDtypeStruct((2 * ker_count, width, (lag_count - late_lags) * width), bf16)
    late_shape = (2 * ker_count, width, late_lags * width)
    late_halves = pltpu.VMEM(late_shape, bf16)
    kernels = in_hbm(kernels)
    early, late, table, wanted = pl.pallas_call(
        functools.partial(prepare_kernel, patch_count),
        in_specs=[HBM] * 3,
        out_specs=[VMEM, HBM, VMEM, VMEM],
        out_shape=[
            early,
            jax.ShapeDtypeStruct((24 * ker_count,) + late_shape[1:], bf16),
            jax.ShapeDtypeStruct((2, interactions.shape[1]), jnp.int32),
            jax.ShapeDtypeStruct((n_recv, width), f32),
        ],
        scratch_shapes=[
            pltpu.VMEM(interactions.shape, jnp.int32),
            pltpu.SMEM(list_lengths.shape, jnp.int32),
            pltpu.VMEM((ker_count, width, lag_count + PAD, width), f32),
            late_halves,
            pltpu.SemaphoreType.DMA((2,)),
            pltpu.SemaphoreType.DMA((ker_count,)),
            pltpu.SemaphoreType.DMA((2 * ker_count,)),
        ],
        compiler_params=grant(46),
        name="prepare",
    )(list_lengths, in_hbm(interactions), kernels)
    late_shape, late = jax.ShapeDtypeStruct(late_shape, bf16), in_hbm(late)
    last_patches = patch_count // 4
    group_sizes = patch_count - last_patches, last_patches
    halves = [
        jax.ShapeDtypeStruct((n_src // 2, size, BLOCK, width), f32)
        for size in group_sizes
        for part in range(2)
    ]
    rates_tail = jax.ShapeDtypeStruct((n_recv, lag_count, width), f32)
    responses_tail = jax.ShapeDtypeStruct((ker_count, n_recv, lag_count, width), f32)
    chunk = min(8, n_recv)
    stress_mib = 16 + 8 * ker_count * n_recv * (lag_count + BLOCK) * width // 2**20
    scratch = [
        pltpu.VMEM((n_recv, lag_count + BLOCK, width), f32),
        pltpu.VMEM((2 * chunk * BLOCK, lag_count * width), bf16),
        pltpu.VMEM((ker_count, n_recv, lag_count + BLOCK, width), f32),
        pltpu.SMEM((2, interactions.shape[1]), jnp.int32),
        pltpu.SemaphoreType.DMA,
    ] + [pltpu.VMEM(((group_rows + 1) * BLOCK, width), f32)] * ker_count

    def reduce_scatter(kept, sent):
        for bit in range(bits):
            pairs = [(i, i ^ (1 << bit)) for i in range(n_src)]
            came = lax.ppermute(sent, "src", pairs)
            if bit == bits - 1:
                return kept, came
            quarter = kept.shape[0] // 2
            sent = kept[quarter:] + came[quarter:]
            kept = kept[:quarter] + came[:quarter]

    rates_group = jax.ShapeDtypeStruct((group_sizes[0], BLOCK, width), f32)

    def solve_first_group(block_idx, terms):
        return pl.pallas_call(
            functools.partial(solve_group_kernel, block_idx),
            in_specs=[VMEM] * 5,
            out_specs=VMEM,
            out_shape=rates_group,
            compiler_params=grant(2),
            name="solve_group",
        )(prestress, friction, load_rate, *terms)

    *totals, rates_tail, responses_tail, late = pl.pallas_call(
        first_stress_kernel,
        in_specs=[VMEM] * 4 + [HBM],
        out_specs=[VMEM] * 7,
        out_shape=halves + [rates_tail, responses_tail, late_shape],
        scratch_shapes=scratch[:3] + [pltpu.SemaphoreType.DMA] + scratch[3:],
        compiler_params=grant(stress_mib),
        name="first_stress",
    )(table, wanted, received, early, late)
    terms = [reduce_scatter(*totals[:2]), reduce_scatter(*totals[2:])]
    second_rates, outgoing = pl.pallas_call(
        middle_block_kernel,
        in_specs=[VMEM] * 7,
        out_specs=[VMEM] * 2,
        out_shape=[
            jax.ShapeDtypeStruct((patch_count, BLOCK, width), f32),
            jax.ShapeDtypeStruct((n_recv, BLOCK, width), f32),
        ],
        compiler_params=grant(4),
        name="middle_block",
    )(received, prestress, friction, load_rate, *terms[1], solve_first_group(1, terms[0]))
    rates = lax.all_to_all(outgoing, "recv", split_axis=0, concat_axis=0, tiled=True)
    totals = pl.pallas_call(
        next_stress_kernel,
        in_specs=[VMEM] * 6,
        out_specs=[VMEM] * 4,
        out_shape=halves,
        scratch_shapes=scratch,
        compiler_params=grant(stress_mib),
        name="next_stress",
    )(table, rates, rates_tail, responses_tail, early, late)
    terms = [reduce_scatter(*totals[:2]), reduce_scatter(*totals[2:])]
    output = pl.pallas_call(
        first_blocks_kernel,
        in_specs=[VMEM] * 4,
        out_specs=HBM,
        out_shape=jax.ShapeDtypeStruct((patch_count, BLOCKS * BLOCK, width), f32),
        scratch_shapes=[
            pltpu.VMEM((patch_count, BLOCK, width), f32),
            pltpu.SemaphoreType.DMA((2,)),
        ],
        compiler_params=grant(4),
        name="first_blocks",
    )(prestress, friction, load_rate, second_rates)
    return pl.pallas_call(
        last_block_kernel,
        in_specs=[VMEM] * 6 + [HBM],
        out_specs=HBM,
        out_shape=jax.ShapeDtypeStruct(output.shape, f32),
        scratch_shapes=[
            pltpu.VMEM((last_patches, BLOCK, width), f32),
            pltpu.SemaphoreType.DMA((last_patches + 1,)),
        ],
        input_output_aliases={6: 0},
        compiler_params=grant(4),
        name="last_block",
    )(
        prestress, friction, load_rate, *terms[1], solve_first_group(2, terms[0]),
        output,
    )


def solution(mesh):
    in_specs = (
        P(None, ("recv", "src")),
        P(("recv", "src")),
        P(("recv", "src"), None, None, None),
        P(("recv", "src"), None),
        P(("recv", "src"), None),
        P(("recv", "src"), None),
    )
    out_specs = P(("recv", "src"), None, None)
    return jax.shard_map(local, mesh=mesh, in_specs=in_specs, out_specs=out_specs, check_vma=False)
```

```python
import functools

import jax
import jax.numpy as jnp
from jax import lax
from jax.experimental import pallas as pl
from jax.experimental.pallas import tpu as pltpu
from jax.sharding import PartitionSpec as P

BLOCK = 32
BLOCKS = 3
NEWTON = 4
PAD = 8
damping = 0.5
def grant(mib):
    return pltpu.CompilerParams(vmem_limit_bytes=mib * 2**20)


VMEM = pl.BlockSpec(memory_space=pltpu.VMEM)
SMEM = pl.BlockSpec(memory_space=pltpu.SMEM)
HBM = pl.BlockSpec(memory_space=pltpu.HBM)


def in_hbm(array):
    return pltpu.with_memory_space_constraint(array, pltpu.HBM)


def friction_solve(drive, friction):
    rates = drive / (damping + friction)
    for newton_step in range(NEWTON - 1):
        squares = 1.0 + rates * rates
        inverse_root = lax.rsqrt(squares)
        magnitude = jnp.log(jnp.abs(rates) + squares * inverse_root)
        inverse_sinh = jnp.where(rates < 0, -magnitude, magnitude)
        misfit = damping * rates + friction * inverse_sinh - drive
        rates = rates - misfit / (damping + friction * inverse_root)
    return rates


def times_of(block_idx, width):
    steps = lax.broadcasted_iota(jnp.int32, (BLOCK, width), 0)
    return (steps + (block_idx * BLOCK + 1)).astype(jnp.float32)


def split(values):
    high = values.astype(jnp.bfloat16)
    return high, (values - high.astype(jnp.float32)).astype(jnp.bfloat16)


def wanted_patches(interactions_ref, slots, patch_count):
    sources = interactions_ref[pl.ds(1, 1), :]
    owners = lax.broadcasted_iota(jnp.int32, (slots, sources.shape[1]), 0)
    first = (owners * lax.axis_size("src") + lax.axis_index("src")) * patch_count
    offset = sources - first
    inside = (offset >= 0) & (offset < patch_count)
    wanted = jnp.max(jnp.where(inside, offset, 0).astype(jnp.float32), axis=1, keepdims=True)
    return owners, inside, wanted


def pack_kernel(interactions_ref, prestress_ref, friction_ref, load_ref, out_ref):
    slots, rows, width = out_ref.shape
    patch_count = prestress_ref.shape[0]
    wanted = wanted_patches(interactions_ref, slots, patch_count)[2]
    wanted = jnp.broadcast_to(wanted, (slots, width))
    for field, ref in enumerate((prestress_ref, friction_ref, load_ref)):
        out_ref[:, field * patch_count : (field + 1) * patch_count, :] = jnp.broadcast_to(
            ref[...][None], (slots, patch_count, width)
        )
    for slot in range(slots):
        out_ref[slot, rows - 1 :, :] = wanted[slot : slot + 1, :]


def split_lag(lag, raw, ker, halves, number):
    width = raw.shape[3]
    rows = raw.reshape(raw.shape[0], width * raw.shape[2], width)
    tile = rows[ker, pl.ds(lag, width, stride=raw.shape[2]), :]
    cols = slice(number * width, (number + 1) * width)
    halves[ker, :, cols], halves[halves.shape[0] // 2 + ker, :, cols] = split(tile)


def prepare_kernel(
    patch_count, lengths_ref, interactions_ref, kernel_ref, early, late_ref, table_ref, wanted_ref,
    interactions, lengths, raw, late, list_sems, load_sems, store_sems,
):
    ker_count, _, lag_count, width = kernel_ref.shape
    early_lags = early.shape[2] // width
    loads = [
        pltpu.make_async_copy(kernel_ref.at[ker], raw.at[ker, :, :lag_count, :], load_sems.at[ker])
        for ker in range(ker_count)
    ]
    list_loads = [
        pltpu.make_async_copy(interactions_ref, interactions, list_sems.at[0]),
        pltpu.make_async_copy(lengths_ref, lengths, list_sems.at[1]),
    ]
    for copy in list_loads + loads:
        copy.start()
    for copy in list_loads:
        copy.wait()

    slots = wanted_ref.shape[0]
    owners, inside, wanted = wanted_patches(interactions, slots, patch_count)
    wanted_ref[...] = jnp.broadcast_to(wanted, wanted_ref.shape)
    n_src = lax.axis_size("src")
    group_rows = n_src * patch_count
    receivers = interactions[pl.ds(0, 1), :] - lax.axis_index("recv") * group_rows
    strips = jnp.zeros_like(receivers)
    for other in range(1, n_src):
        strips = strips + (receivers >= other * patch_count).astype(jnp.int32)
    distance = strips ^ lax.axis_index("src")
    bits = n_src.bit_length() - 1
    order = jnp.zeros_like(distance)
    for bit in range(bits):
        order = order | (((distance >> bit) & 1) << (bits - 1 - bit))
    place = order * patch_count + receivers - strips * patch_count
    entry_numbers = lax.broadcasted_iota(jnp.int32, place.shape, 1)
    place = jnp.where(entry_numbers < lengths[0], place, group_rows)
    table_ref[pl.ds(0, 1), :] = place * BLOCK
    owner = jnp.max(
        jnp.where(inside, owners, 0).astype(jnp.float32), axis=0, keepdims=True
    ).astype(jnp.int32)
    ker_of = jnp.zeros_like(place)
    per_kernel = place.shape[1] // ker_count
    for ker in range(1, ker_count):
        ker_of = ker_of + (entry_numbers >= ker * per_kernel).astype(jnp.int32)
    span = lag_count + BLOCK
    table_ref[pl.ds(1, 1), :] = (
        (ker_of * slots + owner) * span + span - interactions[pl.ds(2, 1), :]
    )

    stores = [
        pltpu.make_async_copy(late.at[part], late_ref.at[part], store_sems.at[part])
        for part in range(2 * ker_count)
    ]
    for ker in range(ker_count):
        loads[ker].wait()
        for lag in range(early_lags, lag_count):
            split_lag(lag, raw, ker, late, lag - early_lags)
        stores[ker].start()
        stores[ker_count + ker].start()
        for lag in range(early_lags):
            split_lag(lag, raw, ker, early, lag)
    for copy in stores:
        copy.wait()


def first_blocks_kernel(
    prestress_ref, friction_ref, load_ref, second_ref, out_ref, rates, sems
):
    patch_count, width = prestress_ref.shape
    second = pltpu.make_async_copy(second_ref, out_ref.at[:, BLOCK : 2 * BLOCK], sems.at[0])
    second.start()
    times = times_of(0, width)
    for patch in range(patch_count):
        row = pl.ds(patch, 1)
        drive = prestress_ref[row, :] + load_ref[row, :] * times
        rates[patch] = friction_solve(drive, jnp.broadcast_to(friction_ref[row, :], drive.shape))
    first = pltpu.make_async_copy(rates, out_ref.at[:, :BLOCK], sems.at[1])
    first.start()
    second.wait()
    first.wait()


def product(left, halves, parts):
    right = jnp.concatenate([halves[part] for part in parts], axis=0)
    return lax.dot_general(
        left, right, (((1,), (1,)), ((), ())), preferred_element_type=jnp.float32
    )


def convolve_and_route(
    window, stacked, responses, sums, early, late, late_copy, table, table_copy, totals
):
    slots, span, width = window.shape
    history = span - BLOCK
    ker_count = responses.shape[0]
    early_lags, late_lags = early.shape[2] // width, late.shape[2] // width
    chunk = stacked.shape[0] // (2 * BLOCK)
    rows = chunk * BLOCK
    chunks = slots // chunk

    def clear():
        for some in sums:
            some[...] = jnp.zeros_like(some)

    if chunks > 1:
        clear()
        if late_copy is not None:
            late_copy.wait()

    def one_chunk(chunk_idx, carry):
        first = chunk_idx * chunk

        for lag in range(early_lags + late_lags):
            cols = slice(lag * width, (lag + 1) * width)
            for slot in range(chunk):
                upper, lower = split(
                    window[first + slot, history - lag : history - lag + BLOCK, :]
                )
                stacked[slot * BLOCK : (slot + 1) * BLOCK, cols] = upper
                stacked[rows + slot * BLOCK : rows + (slot + 1) * BLOCK, cols] = lower
        if chunks == 1:
            clear()

        def part(halves, taps):
            both = product(stacked[:, taps], halves, range(ker_count))
            rest = product(stacked[:rows, taps], halves, range(ker_count, 2 * ker_count))
            return both[:rows] + both[rows:] + rest

        total = part(early, slice(0, early_lags * width))
        if chunks == 1 and late_copy is not None:
            late_copy.wait()
        total = total + part(late, slice(early_lags * width, (early_lags + late_lags) * width))
        for ker in range(ker_count):
            for slot in range(chunk):
                responses[ker, first + slot, history:, :] = total[
                    slot * BLOCK : (slot + 1) * BLOCK, ker * width : (ker + 1) * width
                ]
        return carry

    if chunks == 1:
        one_chunk(0, 0)
    else:
        lax.fori_loop(0, chunks, one_chunk, 0)

    table_copy.wait()
    per_kernel = table.shape[1] // ker_count
    every = responses.reshape(ker_count * slots * span, width)
    for entry in range(per_kernel):
        for ker in range(ker_count):
            idx = ker * per_kernel + entry
            place = pl.ds(pl.multiple_of(table[0, idx], BLOCK), BLOCK)
            some = sums[ker % len(sums)]
            some[place, :] = some[place, :] + every[pl.ds(table[1, idx], BLOCK), :]
    strips = totals[0].shape[0]
    counts = totals[0].shape[1], totals[2].shape[1]
    for group in range(2):
        for part in range(2):
            for strip in range(strips):
                for patch in range(counts[group]):
                    place = (part * strips + strip) * sum(counts) + group * counts[0] + patch
                    rows = slice(place * BLOCK, (place + 1) * BLOCK)
                    total = sums[0][rows, :]
                    for some in sums[1:]:
                        total = total + some[rows, :]
                    totals[2 * group + part][strip, patch] = total


def first_stress_kernel(
    table_ref, wanted_ref, params_ref, early, late_ref,
    *refs,
):
    totals, (rates_tail_ref, responses_tail_ref, late) = refs[:4], refs[4:7]
    window, stacked, responses, late_sem, table, table_sem, *sums = refs[7:]
    table_copy = pltpu.make_async_copy(table_ref, table, table_sem)
    table_copy.start()
    late_copy = pltpu.make_async_copy(late_ref.at[: late.shape[0]], late, late_sem)
    late_copy.start()
    slots, span, width = window.shape
    history = span - BLOCK
    patch_count = (params_ref.shape[1] - 1) // 3
    times = times_of(0, width)
    for ker in range(responses.shape[0]):
        responses[ker, :, :history, :] = jnp.zeros((slots, history, width), jnp.float32)

    patches = lax.broadcasted_iota(jnp.int32, (patch_count, width), 0).astype(jnp.float32)

    def one_slot(slot):
        chosen = patches == wanted_ref[pl.ds(slot, 1), :]

        def field(number):
            rows = params_ref[slot, number * patch_count : (number + 1) * patch_count, :]
            return jnp.sum(jnp.where(chosen, rows, 0.0), axis=0, keepdims=True)

        drive = field(0) + field(2) * times
        friction = jnp.broadcast_to(field(1), drive.shape)
        window[slot, :history, :] = jnp.zeros((history, width), jnp.float32)
        window[slot, history:, :] = friction_solve(drive, friction)

    if slots <= 8:
        for slot in range(slots):
            one_slot(slot)
    else:
        pl.loop(0, slots)(one_slot)
    convolve_and_route(
        window, stacked, responses, sums, early, late, late_copy, table, table_copy, totals
    )
    rates_tail_ref[...] = window[:, BLOCK:, :]
    responses_tail_ref[...] = responses[:, :, BLOCK:, :]


def next_stress_kernel(
    table_ref, rates_ref, rates_tail_ref, responses_tail_ref, early, late,
    *refs,
):
    totals, (window, stacked, responses, table, table_sem, *sums) = refs[:4], refs[4:]
    table_copy = pltpu.make_async_copy(table_ref, table, table_sem)
    table_copy.start()
    history = window.shape[1] - BLOCK
    window[:, :history, :] = rates_tail_ref[...]
    window[:, history:, :] = rates_ref[...]
    responses[:, :, :history, :] = responses_tail_ref[...]
    convolve_and_route(
        window, stacked, responses, sums, early, late, None, table, table_copy, totals
    )


def solve_patch(
    block_idx, patch, first, prestress_ref, friction_ref, load_ref, kept_ref, came_ref
):
    width = prestress_ref.shape[1]
    row = pl.ds(first + patch, 1)
    stress = kept_ref[0, patch] + came_ref[0, patch]
    drive = prestress_ref[row, :] + load_ref[row, :] * times_of(block_idx, width) + stress
    return friction_solve(drive, jnp.broadcast_to(friction_ref[row, :], drive.shape))


def solve_group_kernel(
    block_idx, prestress_ref, friction_ref, load_ref, kept_ref, came_ref, rates_ref
):
    for patch in range(rates_ref.shape[0]):
        rates_ref[patch] = solve_patch(
            block_idx, patch, 0, prestress_ref, friction_ref, load_ref, kept_ref, came_ref
        )


def middle_block_kernel(
    received_ref, prestress_ref, friction_ref, load_ref, kept_ref, came_ref, others_ref,
    rates_ref, outgoing_ref,
):
    known = others_ref.shape[0]
    rates_ref[:known] = others_ref[...]
    for patch in range(rates_ref.shape[0] - known):
        rates_ref[known + patch] = solve_patch(
            1, patch, known, prestress_ref, friction_ref, load_ref, kept_ref, came_ref
        )

    asked_row = received_ref.shape[1] - 1

    def one_slot(slot):
        asked = jnp.broadcast_to(received_ref[slot, asked_row:, :], outgoing_ref.shape[1:])
        chosen = rates_ref[0]
        for patch in range(1, rates_ref.shape[0]):
            chosen = jnp.where(asked == patch, rates_ref[patch], chosen)
        outgoing_ref[slot] = chosen

    slots = outgoing_ref.shape[0]
    if slots <= 8:
        for slot in range(slots):
            one_slot(slot)
    else:
        pl.loop(0, slots)(one_slot)


def last_block_kernel(
    prestress_ref, friction_ref, load_ref, kept_ref, came_ref, others_ref, begun_ref, out_ref,
    rates, sems,
):
    known, patches = others_ref.shape[0], rates.shape[0]
    copies = [
        pltpu.make_async_copy(
            rates.at[patch], out_ref.at[known + patch, 2 * BLOCK :], sems.at[patch]
        )
        for patch in range(patches)
    ]
    others = pltpu.make_async_copy(others_ref, out_ref.at[:known, 2 * BLOCK :], sems.at[patches])
    others.start()
    for patch in range(patches):
        rates[patch] = solve_patch(
            2, patch, known, prestress_ref, friction_ref, load_ref, kept_ref, came_ref
        )
        copies[patch].start()
    for copy in copies + [others]:
        copy.wait()


def local(interactions, list_lengths, kernels, prestress, friction, load_rate):
    n_recv = lax.axis_size("recv")
    n_src = lax.axis_size("src")
    ker_count, width, lag_count, _ = kernels.shape
    patch_count = prestress.shape[0]
    group_rows = n_src * patch_count
    bits = n_src.bit_length() - 1
    assert n_src == 1 << bits and bits > 0

    f32, bf16 = jnp.float32, jnp.bfloat16
    packed = pl.pallas_call(
        pack_kernel,
        in_specs=[VMEM] * 4,
        out_specs=VMEM,
        out_shape=jax.ShapeDtypeStruct((n_recv, 3 * patch_count + 1, width), f32),
        compiler_params=grant(2 + n_recv // 8),
        name="pack",
    )(*map(in_hbm, (interactions, prestress, friction, load_rate)))
    received = lax.all_to_all(packed, "recv", split_axis=0, concat_axis=0, tiled=True)

    late_lags = lag_count // 4
    early = jax.ShapeDtypeStruct((2 * ker_count, width, (lag_count - late_lags) * width), bf16)
    late_shape = (2 * ker_count, width, late_lags * width)
    late_halves = pltpu.VMEM(late_shape, bf16)
    kernels = in_hbm(kernels)
    early, late, table, wanted = pl.pallas_call(
        functools.partial(prepare_kernel, patch_count),
        in_specs=[HBM] * 3,
        out_specs=[VMEM, HBM, VMEM, VMEM],
        out_shape=[
            early,
            jax.ShapeDtypeStruct((24 * ker_count,) + late_shape[1:], bf16),
            jax.ShapeDtypeStruct((2, interactions.shape[1]), jnp.int32),
            jax.ShapeDtypeStruct((n_recv, width), f32),
        ],
        scratch_shapes=[
            pltpu.VMEM(interactions.shape, jnp.int32),
            pltpu.SMEM(list_lengths.shape, jnp.int32),
            pltpu.VMEM((ker_count, width, lag_count + PAD, width), f32),
            late_halves,
            pltpu.SemaphoreType.DMA((2,)),
            pltpu.SemaphoreType.DMA((ker_count,)),
            pltpu.SemaphoreType.DMA((2 * ker_count,)),
        ],
        compiler_params=grant(46),
        name="prepare",
    )(list_lengths, in_hbm(interactions), kernels)
    late_shape, late = jax.ShapeDtypeStruct(late_shape, bf16), in_hbm(late)
    last_patches = patch_count * 3 // 8
    group_sizes = patch_count - last_patches, last_patches
    halves = [
        jax.ShapeDtypeStruct((n_src // 2, size, BLOCK, width), f32)
        for size in group_sizes
        for part in range(2)
    ]
    rates_tail = jax.ShapeDtypeStruct((n_recv, lag_count, width), f32)
    responses_tail = jax.ShapeDtypeStruct((ker_count, n_recv, lag_count, width), f32)
    chunk = min(8, n_recv)
    stress_mib = 16 + 8 * ker_count * n_recv * (lag_count + BLOCK) * width // 2**20
    scratch = [
        pltpu.VMEM((n_recv, lag_count + BLOCK, width), f32),
        pltpu.VMEM((2 * chunk * BLOCK, lag_count * width), bf16),
        pltpu.VMEM((ker_count, n_recv, lag_count + BLOCK, width), f32),
        pltpu.SMEM((2, interactions.shape[1]), jnp.int32),
        pltpu.SemaphoreType.DMA,
    ] + [pltpu.VMEM(((group_rows + 1) * BLOCK, width), f32)] * 2

    def reduce_scatter(kept, sent):
        for bit in range(bits):
            pairs = [(i, i ^ (1 << bit)) for i in range(n_src)]
            came = lax.ppermute(sent, "src", pairs)
            if bit == bits - 1:
                return kept, came
            quarter = kept.shape[0] // 2
            sent = kept[quarter:] + came[quarter:]
            kept = kept[:quarter] + came[:quarter]

    rates_group = jax.ShapeDtypeStruct((group_sizes[0], BLOCK, width), f32)

    def solve_first_group(block_idx, terms):
        return pl.pallas_call(
            functools.partial(solve_group_kernel, block_idx),
            in_specs=[VMEM] * 5,
            out_specs=VMEM,
            out_shape=rates_group,
            compiler_params=grant(2),
            name="solve_group",
        )(prestress, friction, load_rate, *terms)

    *totals, rates_tail, responses_tail, late = pl.pallas_call(
        first_stress_kernel,
        in_specs=[VMEM] * 4 + [HBM],
        out_specs=[VMEM] * 7,
        out_shape=halves + [rates_tail, responses_tail, late_shape],
        scratch_shapes=scratch[:3] + [pltpu.SemaphoreType.DMA] + scratch[3:],
        compiler_params=grant(stress_mib),
        name="first_stress",
    )(table, wanted, received, early, late)
    terms = [reduce_scatter(*totals[:2]), reduce_scatter(*totals[2:])]
    second_rates, outgoing = pl.pallas_call(
        middle_block_kernel,
        in_specs=[VMEM] * 7,
        out_specs=[VMEM] * 2,
        out_shape=[
            jax.ShapeDtypeStruct((patch_count, BLOCK, width), f32),
            jax.ShapeDtypeStruct((n_recv, BLOCK, width), f32),
        ],
        compiler_params=grant(4),
        name="middle_block",
    )(received, prestress, friction, load_rate, *terms[1], solve_first_group(1, terms[0]))
    rates = lax.all_to_all(outgoing, "recv", split_axis=0, concat_axis=0, tiled=True)
    totals = pl.pallas_call(
        next_stress_kernel,
        in_specs=[VMEM] * 6,
        out_specs=[VMEM] * 4,
        out_shape=halves,
        scratch_shapes=scratch,
        compiler_params=grant(stress_mib),
        name="next_stress",
    )(table, rates, rates_tail, responses_tail, early, late)
    terms = [reduce_scatter(*totals[:2]), reduce_scatter(*totals[2:])]
    output = pl.pallas_call(
        first_blocks_kernel,
        in_specs=[VMEM] * 4,
        out_specs=HBM,
        out_shape=jax.ShapeDtypeStruct((patch_count, BLOCKS * BLOCK, width), f32),
        scratch_shapes=[
            pltpu.VMEM((patch_count, BLOCK, width), f32),
            pltpu.SemaphoreType.DMA((2,)),
        ],
        compiler_params=grant(4),
        name="first_blocks",
    )(prestress, friction, load_rate, second_rates)
    return pl.pallas_call(
        last_block_kernel,
        in_specs=[VMEM] * 6 + [HBM],
        out_specs=HBM,
        out_shape=jax.ShapeDtypeStruct(output.shape, f32),
        scratch_shapes=[
            pltpu.VMEM((last_patches, BLOCK, width), f32),
            pltpu.SemaphoreType.DMA((last_patches + 1,)),
        ],
        input_output_aliases={6: 0},
        compiler_params=grant(4),
        name="last_block",
    )(
        prestress, friction, load_rate, *terms[1], solve_first_group(2, terms[0]),
        output,
    )


def solution(mesh):
    in_specs = (
        P(None, ("recv", "src")),
        P(("recv", "src")),
        P(("recv", "src"), None, None, None),
        P(("recv", "src"), None),
        P(("recv", "src"), None),
        P(("recv", "src"), None),
    )
    out_specs = P(("recv", "src"), None, None)
    return jax.shard_map(local, mesh=mesh, in_specs=in_specs, out_specs=out_specs, check_vma=False)
```

```python
import functools

import jax
import jax.numpy as jnp
from jax import lax
from jax.experimental import pallas as pl
from jax.experimental.pallas import tpu as pltpu
from jax.sharding import PartitionSpec as P

BLOCK = 32
BLOCKS = 3
NEWTON = 4
PAD = 8
damping = 0.5
def grant(mib):
    return pltpu.CompilerParams(vmem_limit_bytes=mib * 2**20)


VMEM = pl.BlockSpec(memory_space=pltpu.VMEM)
SMEM = pl.BlockSpec(memory_space=pltpu.SMEM)
HBM = pl.BlockSpec(memory_space=pltpu.HBM)


def in_hbm(array):
    return pltpu.with_memory_space_constraint(array, pltpu.HBM)


def friction_solve(drive, friction):
    rates = drive / (damping + friction)
    for newton_step in range(NEWTON - 1):
        squares = 1.0 + rates * rates
        inverse_root = lax.rsqrt(squares)
        magnitude = jnp.log(jnp.abs(rates) + squares * inverse_root)
        inverse_sinh = jnp.where(rates < 0, -magnitude, magnitude)
        rates = (drive + friction * (rates * inverse_root - inverse_sinh)) / (
            damping + friction * inverse_root
        )
    return rates


def times_of(block_idx, width):
    steps = lax.broadcasted_iota(jnp.int32, (BLOCK, width), 0)
    return (steps + (block_idx * BLOCK + 1)).astype(jnp.float32)


def split(values):
    high = values.astype(jnp.bfloat16)
    return high, (values - high.astype(jnp.float32)).astype(jnp.bfloat16)


def wanted_patches(interactions_ref, slots, patch_count):
    sources = interactions_ref[pl.ds(1, 1), :]
    owners = lax.broadcasted_iota(jnp.int32, (slots, sources.shape[1]), 0)
    first = (owners * lax.axis_size("src") + lax.axis_index("src")) * patch_count
    offset = sources - first
    inside = (offset >= 0) & (offset < patch_count)
    wanted = jnp.max(jnp.where(inside, offset, 0).astype(jnp.float32), axis=1, keepdims=True)
    return owners, inside, wanted


def pack_kernel(interactions_ref, prestress_ref, friction_ref, load_ref, out_ref):
    slots, rows, width = out_ref.shape
    patch_count = prestress_ref.shape[0]
    wanted = wanted_patches(interactions_ref, slots, patch_count)[2]
    wanted = jnp.broadcast_to(wanted, (slots, width))
    for field, ref in enumerate((prestress_ref, friction_ref, load_ref)):
        out_ref[:, field * patch_count : (field + 1) * patch_count, :] = jnp.broadcast_to(
            ref[...][None], (slots, patch_count, width)
        )
    for slot in range(slots):
        out_ref[slot, rows - 1 :, :] = wanted[slot : slot + 1, :]


def split_lag(lag, raw, ker, halves, number):
    width = raw.shape[3]
    rows = raw.reshape(raw.shape[0], width * raw.shape[2], width)
    tile = rows[ker, pl.ds(lag, width, stride=raw.shape[2]), :]
    cols = slice(number * width, (number + 1) * width)
    halves[ker, :, cols], halves[halves.shape[0] // 2 + ker, :, cols] = split(tile)


def prepare_kernel(
    patch_count, lengths_ref, interactions_ref, kernel_ref, early, late_ref, table_ref, wanted_ref,
    interactions, lengths, raw, late, list_sems, load_sems, store_sems,
):
    ker_count, _, lag_count, width = kernel_ref.shape
    early_lags = early.shape[2] // width
    loads = [
        pltpu.make_async_copy(kernel_ref.at[ker], raw.at[ker, :, :lag_count, :], load_sems.at[ker])
        for ker in range(ker_count)
    ]
    list_loads = [
        pltpu.make_async_copy(interactions_ref, interactions, list_sems.at[0]),
        pltpu.make_async_copy(lengths_ref, lengths, list_sems.at[1]),
    ]
    for copy in list_loads + loads:
        copy.start()
    for copy in list_loads:
        copy.wait()

    slots = wanted_ref.shape[0]
    owners, inside, wanted = wanted_patches(interactions, slots, patch_count)
    wanted_ref[...] = jnp.broadcast_to(wanted, wanted_ref.shape)
    n_src = lax.axis_size("src")
    group_rows = n_src * patch_count
    receivers = interactions[pl.ds(0, 1), :] - lax.axis_index("recv") * group_rows
    strips = jnp.zeros_like(receivers)
    for other in range(1, n_src):
        strips = strips + (receivers >= other * patch_count).astype(jnp.int32)
    distance = strips ^ lax.axis_index("src")
    bits = n_src.bit_length() - 1
    order = jnp.zeros_like(distance)
    for bit in range(bits):
        order = order | (((distance >> bit) & 1) << (bits - 1 - bit))
    place = order * patch_count + receivers - strips * patch_count
    entry_numbers = lax.broadcasted_iota(jnp.int32, place.shape, 1)
    place = jnp.where(entry_numbers < lengths[0], place, group_rows)
    table_ref[pl.ds(0, 1), :] = place * BLOCK
    owner = jnp.max(
        jnp.where(inside, owners, 0).astype(jnp.float32), axis=0, keepdims=True
    ).astype(jnp.int32)
    ker_of = jnp.zeros_like(place)
    per_kernel = place.shape[1] // ker_count
    for ker in range(1, ker_count):
        ker_of = ker_of + (entry_numbers >= ker * per_kernel).astype(jnp.int32)
    span = lag_count + BLOCK
    table_ref[pl.ds(1, 1), :] = (
        (ker_of * slots + owner) * span + span - interactions[pl.ds(2, 1), :]
    )

    stores = [
        pltpu.make_async_copy(late.at[part], late_ref.at[part], store_sems.at[part])
        for part in range(2 * ker_count)
    ]
    for ker in range(ker_count):
        loads[ker].wait()
        for lag in range(early_lags, lag_count):
            split_lag(lag, raw, ker, late, lag - early_lags)
        stores[ker].start()
        stores[ker_count + ker].start()
        for lag in range(early_lags):
            split_lag(lag, raw, ker, early, lag)
    for copy in stores:
        copy.wait()


def first_blocks_kernel(
    prestress_ref, friction_ref, load_ref, second_ref, out_ref, rates, sems
):
    patch_count, width = prestress_ref.shape
    second = pltpu.make_async_copy(second_ref, out_ref.at[:, BLOCK : 2 * BLOCK], sems.at[0])
    second.start()
    times = times_of(0, width)
    for patch in range(patch_count):
        row = pl.ds(patch, 1)
        drive = prestress_ref[row, :] + load_ref[row, :] * times
        rates[patch] = friction_solve(drive, jnp.broadcast_to(friction_ref[row, :], drive.shape))
    first = pltpu.make_async_copy(rates, out_ref.at[:, :BLOCK], sems.at[1])
    first.start()
    second.wait()
    first.wait()


def product(left, halves, parts):
    right = jnp.concatenate([halves[part] for part in parts], axis=0)
    return lax.dot_general(
        left, right, (((1,), (1,)), ((), ())), preferred_element_type=jnp.float32
    )


def convolve_and_route(
    window, stacked, responses, sums, early, late, late_copy, table, table_copy, totals
):
    slots, span, width = window.shape
    history = span - BLOCK
    ker_count = responses.shape[0]
    early_lags, late_lags = early.shape[2] // width, late.shape[2] // width
    chunk = stacked.shape[0] // (2 * BLOCK)
    rows = chunk * BLOCK
    chunks = slots // chunk

    def clear():
        for ker in range(ker_count):
            sums[ker][...] = jnp.zeros_like(sums[ker])

    if chunks > 1:
        clear()
        if late_copy is not None:
            late_copy.wait()

    def one_chunk(chunk_idx, carry):
        first = chunk_idx * chunk

        for lag in range(early_lags + late_lags):
            cols = slice(lag * width, (lag + 1) * width)
            for slot in range(chunk):
                upper, lower = split(
                    window[first + slot, history - lag : history - lag + BLOCK, :]
                )
                stacked[slot * BLOCK : (slot + 1) * BLOCK, cols] = upper
                stacked[rows + slot * BLOCK : rows + (slot + 1) * BLOCK, cols] = lower
        if chunks == 1:
            clear()

        def part(halves, taps):
            both = product(stacked[:, taps], halves, range(ker_count))
            rest = product(stacked[:rows, taps], halves, range(ker_count, 2 * ker_count))
            return both[:rows] + both[rows:] + rest

        total = part(early, slice(0, early_lags * width))
        if chunks == 1 and late_copy is not None:
            late_copy.wait()
        total = total + part(late, slice(early_lags * width, (early_lags + late_lags) * width))
        for ker in range(ker_count):
            for slot in range(chunk):
                responses[ker, first + slot, history:, :] = total[
                    slot * BLOCK : (slot + 1) * BLOCK, ker * width : (ker + 1) * width
                ]
        return carry

    if chunks == 1:
        one_chunk(0, 0)
    else:
        lax.fori_loop(0, chunks, one_chunk, 0)

    table_copy.wait()
    per_kernel = table.shape[1] // ker_count
    every = responses.reshape(ker_count * slots * span, width)
    for entry in range(per_kernel):
        for ker in range(ker_count):
            idx = ker * per_kernel + entry
            place = pl.ds(pl.multiple_of(table[0, idx], BLOCK), BLOCK)
            sums[ker][place, :] = sums[ker][place, :] + every[pl.ds(table[1, idx], BLOCK), :]
    strips = totals[0].shape[0]
    counts = totals[0].shape[1], totals[2].shape[1]
    for group in range(2):
        for part in range(2):
            for strip in range(strips):
                for patch in range(counts[group]):
                    place = (part * strips + strip) * sum(counts) + group * counts[0] + patch
                    rows = slice(place * BLOCK, (place + 1) * BLOCK)
                    total = sums[0][rows, :]
                    for ker in range(1, ker_count):
                        total = total + sums[ker][rows, :]
                    totals[2 * group + part][strip, patch] = total


def first_stress_kernel(
    table_ref, wanted_ref, params_ref, early, late_ref,
    *refs,
):
    totals, (rates_tail_ref, responses_tail_ref, late) = refs[:4], refs[4:7]
    window, stacked, responses, late_sem, table, table_sem, *sums = refs[7:]
    table_copy = pltpu.make_async_copy(table_ref, table, table_sem)
    table_copy.start()
    late_copy = pltpu.make_async_copy(late_ref.at[: late.shape[0]], late, late_sem)
    late_copy.start()
    slots, span, width = window.shape
    history = span - BLOCK
    patch_count = (params_ref.shape[1] - 1) // 3
    times = times_of(0, width)
    for ker in range(responses.shape[0]):
        responses[ker, :, :history, :] = jnp.zeros((slots, history, width), jnp.float32)

    patches = lax.broadcasted_iota(jnp.int32, (patch_count, width), 0).astype(jnp.float32)

    def one_slot(slot):
        chosen = patches == wanted_ref[pl.ds(slot, 1), :]

        def field(number):
            rows = params_ref[slot, number * patch_count : (number + 1) * patch_count, :]
            return jnp.sum(jnp.where(chosen, rows, 0.0), axis=0, keepdims=True)

        drive = field(0) + field(2) * times
        friction = jnp.broadcast_to(field(1), drive.shape)
        window[slot, :history, :] = jnp.zeros((history, width), jnp.float32)
        window[slot, history:, :] = friction_solve(drive, friction)

    if slots <= 8:
        for slot in range(slots):
            one_slot(slot)
    else:
        pl.loop(0, slots)(one_slot)
    convolve_and_route(
        window, stacked, responses, sums, early, late, late_copy, table, table_copy, totals
    )
    rates_tail_ref[...] = window[:, BLOCK:, :]
    responses_tail_ref[...] = responses[:, :, BLOCK:, :]


def next_stress_kernel(
    table_ref, rates_ref, rates_tail_ref, responses_tail_ref, early, late,
    *refs,
):
    totals, (window, stacked, responses, table, table_sem, *sums) = refs[:4], refs[4:]
    table_copy = pltpu.make_async_copy(table_ref, table, table_sem)
    table_copy.start()
    history = window.shape[1] - BLOCK
    window[:, :history, :] = rates_tail_ref[...]
    window[:, history:, :] = rates_ref[...]
    responses[:, :, :history, :] = responses_tail_ref[...]
    convolve_and_route(
        window, stacked, responses, sums, early, late, None, table, table_copy, totals
    )


def solve_patch(
    block_idx, patch, first, prestress_ref, friction_ref, load_ref, kept_ref, came_ref
):
    width = prestress_ref.shape[1]
    row = pl.ds(first + patch, 1)
    stress = kept_ref[0, patch] + came_ref[0, patch]
    drive = prestress_ref[row, :] + load_ref[row, :] * times_of(block_idx, width) + stress
    return friction_solve(drive, jnp.broadcast_to(friction_ref[row, :], drive.shape))


def solve_group_kernel(
    block_idx, prestress_ref, friction_ref, load_ref, kept_ref, came_ref, rates_ref
):
    for patch in range(rates_ref.shape[0]):
        rates_ref[patch] = solve_patch(
            block_idx, patch, 0, prestress_ref, friction_ref, load_ref, kept_ref, came_ref
        )


def middle_block_kernel(
    received_ref, prestress_ref, friction_ref, load_ref, kept_ref, came_ref, others_ref,
    rates_ref, outgoing_ref,
):
    known = others_ref.shape[0]
    rates_ref[:known] = others_ref[...]
    for patch in range(rates_ref.shape[0] - known):
        rates_ref[known + patch] = solve_patch(
            1, patch, known, prestress_ref, friction_ref, load_ref, kept_ref, came_ref
        )

    asked_row = received_ref.shape[1] - 1

    def one_slot(slot):
        asked = jnp.broadcast_to(received_ref[slot, asked_row:, :], outgoing_ref.shape[1:])
        chosen = rates_ref[0]
        for patch in range(1, rates_ref.shape[0]):
            chosen = jnp.where(asked == patch, rates_ref[patch], chosen)
        outgoing_ref[slot] = chosen

    slots = outgoing_ref.shape[0]
    if slots <= 8:
        for slot in range(slots):
            one_slot(slot)
    else:
        pl.loop(0, slots)(one_slot)


def last_block_kernel(
    prestress_ref, friction_ref, load_ref, kept_ref, came_ref, others_ref, begun_ref, out_ref,
    rates, sems,
):
    known, patches = others_ref.shape[0], rates.shape[0]
    copies = [
        pltpu.make_async_copy(
            rates.at[patch], out_ref.at[known + patch, 2 * BLOCK :], sems.at[patch]
        )
        for patch in range(patches)
    ]
    others = pltpu.make_async_copy(others_ref, out_ref.at[:known, 2 * BLOCK :], sems.at[patches])
    others.start()
    for patch in range(patches):
        rates[patch] = solve_patch(
            2, patch, known, prestress_ref, friction_ref, load_ref, kept_ref, came_ref
        )
        copies[patch].start()
    for copy in copies + [others]:
        copy.wait()


def local(interactions, list_lengths, kernels, prestress, friction, load_rate):
    n_recv = lax.axis_size("recv")
    n_src = lax.axis_size("src")
    ker_count, width, lag_count, _ = kernels.shape
    patch_count = prestress.shape[0]
    group_rows = n_src * patch_count
    bits = n_src.bit_length() - 1
    assert n_src == 1 << bits and bits > 0

    f32, bf16 = jnp.float32, jnp.bfloat16
    packed = pl.pallas_call(
        pack_kernel,
        in_specs=[VMEM] * 4,
        out_specs=VMEM,
        out_shape=jax.ShapeDtypeStruct((n_recv, 3 * patch_count + 1, width), f32),
        compiler_params=grant(2 + n_recv // 8),
        name="pack",
    )(*map(in_hbm, (interactions, prestress, friction, load_rate)))
    received = lax.all_to_all(packed, "recv", split_axis=0, concat_axis=0, tiled=True)

    late_lags = lag_count // 4
    early = jax.ShapeDtypeStruct((2 * ker_count, width, (lag_count - late_lags) * width), bf16)
    late_shape = (2 * ker_count, width, late_lags * width)
    late_halves = pltpu.VMEM(late_shape, bf16)
    kernels = in_hbm(kernels)
    early, late, table, wanted = pl.pallas_call(
        functools.partial(prepare_kernel, patch_count),
        in_specs=[HBM] * 3,
        out_specs=[VMEM, HBM, VMEM, VMEM],
        out_shape=[
            early,
            jax.ShapeDtypeStruct((24 * ker_count,) + late_shape[1:], bf16),
            jax.ShapeDtypeStruct((2, interactions.shape[1]), jnp.int32),
            jax.ShapeDtypeStruct((n_recv, width), f32),
        ],
        scratch_shapes=[
            pltpu.VMEM(interactions.shape, jnp.int32),
            pltpu.SMEM(list_lengths.shape, jnp.int32),
            pltpu.VMEM((ker_count, width, lag_count + PAD, width), f32),
            late_halves,
            pltpu.SemaphoreType.DMA((2,)),
            pltpu.SemaphoreType.DMA((ker_count,)),
            pltpu.SemaphoreType.DMA((2 * ker_count,)),
        ],
        compiler_params=grant(46),
        name="prepare",
    )(list_lengths, in_hbm(interactions), kernels)
    late_shape, late = jax.ShapeDtypeStruct(late_shape, bf16), in_hbm(late)
    last_patches = patch_count // 4
    group_sizes = patch_count - last_patches, last_patches
    halves = [
        jax.ShapeDtypeStruct((n_src // 2, size, BLOCK, width), f32)
        for size in group_sizes
        for part in range(2)
    ]
    rates_tail = jax.ShapeDtypeStruct((n_recv, lag_count, width), f32)
    responses_tail = jax.ShapeDtypeStruct((ker_count, n_recv, lag_count, width), f32)
    chunk = min(8, n_recv)
    stress_mib = 16 + 8 * ker_count * n_recv * (lag_count + BLOCK) * width // 2**20
    scratch = [
        pltpu.VMEM((n_recv, lag_count + BLOCK, width), f32),
        pltpu.VMEM((2 * chunk * BLOCK, lag_count * width), bf16),
        pltpu.VMEM((ker_count, n_recv, lag_count + BLOCK, width), f32),
        pltpu.SMEM((2, interactions.shape[1]), jnp.int32),
        pltpu.SemaphoreType.DMA,
    ] + [pltpu.VMEM(((group_rows + 1) * BLOCK, width), f32)] * ker_count

    def reduce_scatter(kept, sent):
        for bit in range(bits):
            pairs = [(i, i ^ (1 << bit)) for i in range(n_src)]
            came = lax.ppermute(sent, "src", pairs)
            if bit == bits - 1:
                return kept, came
            quarter = kept.shape[0] // 2
            sent = kept[quarter:] + came[quarter:]
            kept = kept[:quarter] + came[:quarter]

    rates_group = jax.ShapeDtypeStruct((group_sizes[0], BLOCK, width), f32)

    def solve_first_group(block_idx, terms):
        return pl.pallas_call(
            functools.partial(solve_group_kernel, block_idx),
            in_specs=[VMEM] * 5,
            out_specs=VMEM,
            out_shape=rates_group,
            compiler_params=grant(2),
            name="solve_group",
        )(prestress, friction, load_rate, *terms)

    *totals, rates_tail, responses_tail, late = pl.pallas_call(
        first_stress_kernel,
        in_specs=[VMEM] * 4 + [HBM],
        out_specs=[VMEM] * 7,
        out_shape=halves + [rates_tail, responses_tail, late_shape],
        scratch_shapes=scratch[:3] + [pltpu.SemaphoreType.DMA] + scratch[3:],
        compiler_params=grant(stress_mib),
        name="first_stress",
    )(table, wanted, received, early, late)
    terms = [reduce_scatter(*totals[:2]), reduce_scatter(*totals[2:])]
    second_rates, outgoing = pl.pallas_call(
        middle_block_kernel,
        in_specs=[VMEM] * 7,
        out_specs=[VMEM] * 2,
        out_shape=[
            jax.ShapeDtypeStruct((patch_count, BLOCK, width), f32),
            jax.ShapeDtypeStruct((n_recv, BLOCK, width), f32),
        ],
        compiler_params=grant(4),
        name="middle_block",
    )(received, prestress, friction, load_rate, *terms[1], solve_first_group(1, terms[0]))
    rates = lax.all_to_all(outgoing, "recv", split_axis=0, concat_axis=0, tiled=True)
    totals = pl.pallas_call(
        next_stress_kernel,
        in_specs=[VMEM] * 6,
        out_specs=[VMEM] * 4,
        out_shape=halves,
        scratch_shapes=scratch,
        compiler_params=grant(stress_mib),
        name="next_stress",
    )(table, rates, rates_tail, responses_tail, early, late)
    terms = [reduce_scatter(*totals[:2]), reduce_scatter(*totals[2:])]
    output = pl.pallas_call(
        first_blocks_kernel,
        in_specs=[VMEM] * 4,
        out_specs=HBM,
        out_shape=jax.ShapeDtypeStruct((patch_count, BLOCKS * BLOCK, width), f32),
        scratch_shapes=[
            pltpu.VMEM((patch_count, BLOCK, width), f32),
            pltpu.SemaphoreType.DMA((2,)),
        ],
        compiler_params=grant(4),
        name="first_blocks",
    )(prestress, friction, load_rate, second_rates)
    return pl.pallas_call(
        last_block_kernel,
        in_specs=[VMEM] * 6 + [HBM],
        out_specs=HBM,
        out_shape=jax.ShapeDtypeStruct(output.shape, f32),
        scratch_shapes=[
            pltpu.VMEM((last_patches, BLOCK, width), f32),
            pltpu.SemaphoreType.DMA((last_patches + 1,)),
        ],
        input_output_aliases={6: 0},
        compiler_params=grant(4),
        name="last_block",
    )(
        prestress, friction, load_rate, *terms[1], solve_first_group(2, terms[0]),
        output,
    )


def solution(mesh):
    in_specs = (
        P(None, ("recv", "src")),
        P(("recv", "src")),
        P(("recv", "src"), None, None, None),
        P(("recv", "src"), None),
        P(("recv", "src"), None),
        P(("recv", "src"), None),
    )
    out_specs = P(("recv", "src"), None, None)
    return jax.shard_map(local, mesh=mesh, in_specs=in_specs, out_specs=out_specs, check_vma=False)
```

```python
import functools

import jax
import jax.numpy as jnp
from jax import lax
from jax.experimental import pallas as pl
from jax.experimental.pallas import tpu as pltpu
from jax.sharding import PartitionSpec as P

BLOCK = 32
BLOCKS = 3
NEWTON = 4
PAD = 8
damping = 0.5
def grant(mib):
    return pltpu.CompilerParams(vmem_limit_bytes=mib * 2**20)


VMEM = pl.BlockSpec(memory_space=pltpu.VMEM)
SMEM = pl.BlockSpec(memory_space=pltpu.SMEM)
HBM = pl.BlockSpec(memory_space=pltpu.HBM)


def in_hbm(array):
    return pltpu.with_memory_space_constraint(array, pltpu.HBM)


def friction_solve(drive, friction):
    rates = drive / (damping + friction)
    for newton_step in range(NEWTON - 1):
        squares = 1.0 + rates * rates
        inverse_root = lax.rsqrt(squares)
        magnitude = jnp.log(jnp.abs(rates) + squares * inverse_root)
        inverse_sinh = jnp.where(rates < 0, -magnitude, magnitude)
        rates = (drive + friction * (rates * inverse_root - inverse_sinh)) / (
            damping + friction * inverse_root
        )
    return rates


def times_of(block_idx, width):
    steps = lax.broadcasted_iota(jnp.int32, (BLOCK, width), 0)
    return (steps + (block_idx * BLOCK + 1)).astype(jnp.float32)


def split(values):
    high = values.astype(jnp.bfloat16)
    return high, (values - high.astype(jnp.float32)).astype(jnp.bfloat16)


def wanted_patches(interactions_ref, slots, patch_count):
    sources = interactions_ref[pl.ds(1, 1), :]
    owners = lax.broadcasted_iota(jnp.int32, (slots, sources.shape[1]), 0)
    first = (owners * lax.axis_size("src") + lax.axis_index("src")) * patch_count
    offset = sources - first
    inside = (offset >= 0) & (offset < patch_count)
    wanted = jnp.max(jnp.where(inside, offset, 0).astype(jnp.float32), axis=1, keepdims=True)
    return owners, inside, wanted


def pack_kernel(interactions_ref, prestress_ref, friction_ref, load_ref, out_ref):
    slots, rows, width = out_ref.shape
    patch_count = prestress_ref.shape[0]
    wanted = wanted_patches(interactions_ref, slots, patch_count)[2]
    wanted = jnp.broadcast_to(wanted, (slots, width))
    for field, ref in enumerate((prestress_ref, friction_ref, load_ref)):
        out_ref[:, field * patch_count : (field + 1) * patch_count, :] = jnp.broadcast_to(
            ref[...][None], (slots, patch_count, width)
        )
    for slot in range(slots):
        out_ref[slot, rows - 1 :, :] = wanted[slot : slot + 1, :]


def split_lag(lag, raw, ker, halves, number):
    width = raw.shape[3]
    rows = raw.reshape(raw.shape[0], width * raw.shape[2], width)
    tile = rows[ker, pl.ds(lag, width, stride=raw.shape[2]), :]
    cols = slice(number * width, (number + 1) * width)
    halves[ker, :, cols], halves[halves.shape[0] // 2 + ker, :, cols] = split(tile)


def prepare_kernel(
    patch_count, lengths_ref, interactions_ref, kernel_ref, early, late_ref, table_ref, wanted_ref,
    interactions, lengths, raw, late, list_sems, load_sems, store_sems,
):
    ker_count, _, lag_count, width = kernel_ref.shape
    early_lags = early.shape[2] // width
    loads = [
        pltpu.make_async_copy(kernel_ref.at[ker], raw.at[ker, :, :lag_count, :], load_sems.at[ker])
        for ker in range(ker_count)
    ]
    list_loads = [
        pltpu.make_async_copy(interactions_ref, interactions, list_sems.at[0]),
        pltpu.make_async_copy(lengths_ref, lengths, list_sems.at[1]),
    ]
    for copy in list_loads + loads:
        copy.start()
    for copy in list_loads:
        copy.wait()

    slots = wanted_ref.shape[0]
    owners, inside, wanted = wanted_patches(interactions, slots, patch_count)
    wanted_ref[...] = jnp.broadcast_to(wanted, wanted_ref.shape)
    n_src = lax.axis_size("src")
    group_rows = n_src * patch_count
    receivers = interactions[pl.ds(0, 1), :] - lax.axis_index("recv") * group_rows
    strips = jnp.zeros_like(receivers)
    for other in range(1, n_src):
        strips = strips + (receivers >= other * patch_count).astype(jnp.int32)
    distance = strips ^ lax.axis_index("src")
    bits = n_src.bit_length() - 1
    order = jnp.zeros_like(distance)
    for bit in range(bits):
        order = order | (((distance >> bit) & 1) << (bits - 1 - bit))
    place = order * patch_count + receivers - strips * patch_count
    entry_numbers = lax.broadcasted_iota(jnp.int32, place.shape, 1)
    place = jnp.where(entry_numbers < lengths[0], place, group_rows)
    table_ref[pl.ds(0, 1), :] = place * BLOCK
    owner = jnp.max(
        jnp.where(inside, owners, 0).astype(jnp.float32), axis=0, keepdims=True
    ).astype(jnp.int32)
    ker_of = jnp.zeros_like(place)
    per_kernel = place.shape[1] // ker_count
    for ker in range(1, ker_count):
        ker_of = ker_of + (entry_numbers >= ker * per_kernel).astype(jnp.int32)
    span = lag_count + BLOCK
    table_ref[pl.ds(1, 1), :] = (
        (ker_of * slots + owner) * span + span - interactions[pl.ds(2, 1), :]
    )

    stores = [
        pltpu.make_async_copy(late.at[part], late_ref.at[part], store_sems.at[part])
        for part in range(2 * ker_count)
    ]
    for ker in range(ker_count):
        loads[ker].wait()
        for lag in range(early_lags, lag_count):
            split_lag(lag, raw, ker, late, lag - early_lags)
        stores[ker].start()
        stores[ker_count + ker].start()
        for lag in range(early_lags):
            split_lag(lag, raw, ker, early, lag)
    for copy in stores:
        copy.wait()


def first_blocks_kernel(
    prestress_ref, friction_ref, load_ref, second_ref, out_ref, rates, sems
):
    patch_count, width = prestress_ref.shape
    second = pltpu.make_async_copy(second_ref, out_ref.at[:, BLOCK : 2 * BLOCK], sems.at[0])
    second.start()
    times = times_of(0, width)
    for patch in range(patch_count):
        row = pl.ds(patch, 1)
        drive = prestress_ref[row, :] + load_ref[row, :] * times
        rates[patch] = friction_solve(drive, jnp.broadcast_to(friction_ref[row, :], drive.shape))
    first = pltpu.make_async_copy(rates, out_ref.at[:, :BLOCK], sems.at[1])
    first.start()
    second.wait()
    first.wait()


def product(left, halves, parts):
    right = jnp.concatenate([halves[part] for part in parts], axis=0)
    return lax.dot_general(
        left, right, (((1,), (1,)), ((), ())), preferred_element_type=jnp.float32
    )


def convolve_and_route(
    window, stacked, responses, sums, early, late, late_copy, table, table_copy, totals
):
    slots, span, width = window.shape
    history = span - BLOCK
    ker_count = responses.shape[0]
    early_lags, late_lags = early.shape[2] // width, late.shape[2] // width
    chunk = stacked.shape[0] // (2 * BLOCK)
    rows = chunk * BLOCK
    chunks = slots // chunk

    def clear():
        for some in sums:
            some[...] = jnp.zeros_like(some)

    if chunks > 1:
        clear()
        if late_copy is not None:
            late_copy.wait()

    def one_chunk(chunk_idx, carry):
        first = chunk_idx * chunk

        for lag in range(early_lags + late_lags):
            cols = slice(lag * width, (lag + 1) * width)
            for slot in range(chunk):
                upper, lower = split(
                    window[first + slot, history - lag : history - lag + BLOCK, :]
                )
                stacked[slot * BLOCK : (slot + 1) * BLOCK, cols] = upper
                stacked[rows + slot * BLOCK : rows + (slot + 1) * BLOCK, cols] = lower
        if chunks == 1:
            clear()

        def part(halves, taps):
            both = product(stacked[:, taps], halves, range(ker_count))
            rest = product(stacked[:rows, taps], halves, range(ker_count, 2 * ker_count))
            return both[:rows] + both[rows:] + rest

        total = part(early, slice(0, early_lags * width))
        if chunks == 1 and late_copy is not None:
            late_copy.wait()
        total = total + part(late, slice(early_lags * width, (early_lags + late_lags) * width))
        for ker in range(ker_count):
            for slot in range(chunk):
                responses[ker, first + slot, history:, :] = total[
                    slot * BLOCK : (slot + 1) * BLOCK, ker * width : (ker + 1) * width
                ]
        return carry

    if chunks == 1:
        one_chunk(0, 0)
    else:
        lax.fori_loop(0, chunks, one_chunk, 0)

    table_copy.wait()
    per_kernel = table.shape[1] // ker_count
    every = responses.reshape(ker_count * slots * span, width)
    for entry in range(per_kernel):
        for ker in range(ker_count):
            idx = ker * per_kernel + entry
            place = pl.ds(pl.multiple_of(table[0, idx], BLOCK), BLOCK)
            some = sums[ker % len(sums)]
            some[place, :] = some[place, :] + every[pl.ds(table[1, idx], BLOCK), :]
    strips = totals[0].shape[0]
    counts = totals[0].shape[1], totals[2].shape[1]
    for group in range(2):
        for part in range(2):
            for strip in range(strips):
                for patch in range(counts[group]):
                    place = (part * strips + strip) * sum(counts) + group * counts[0] + patch
                    rows = slice(place * BLOCK, (place + 1) * BLOCK)
                    total = sums[0][rows, :]
                    for some in sums[1:]:
                        total = total + some[rows, :]
                    totals[2 * group + part][strip, patch] = total


def first_stress_kernel(
    table_ref, wanted_ref, params_ref, early, late_ref,
    *refs,
):
    totals, (rates_tail_ref, responses_tail_ref, late) = refs[:4], refs[4:7]
    window, stacked, responses, late_sem, table, table_sem, *sums = refs[7:]
    table_copy = pltpu.make_async_copy(table_ref, table, table_sem)
    table_copy.start()
    late_copy = pltpu.make_async_copy(late_ref.at[: late.shape[0]], late, late_sem)
    late_copy.start()
    slots, span, width = window.shape
    history = span - BLOCK
    patch_count = (params_ref.shape[1] - 1) // 3
    times = times_of(0, width)
    for ker in range(responses.shape[0]):
        responses[ker, :, :history, :] = jnp.zeros((slots, history, width), jnp.float32)

    patches = lax.broadcasted_iota(jnp.int32, (patch_count, width), 0).astype(jnp.float32)

    def one_slot(slot):
        chosen = patches == wanted_ref[pl.ds(slot, 1), :]

        def field(number):
            rows = params_ref[slot, number * patch_count : (number + 1) * patch_count, :]
            return jnp.sum(jnp.where(chosen, rows, 0.0), axis=0, keepdims=True)

        drive = field(0) + field(2) * times
        friction = jnp.broadcast_to(field(1), drive.shape)
        window[slot, :history, :] = jnp.zeros((history, width), jnp.float32)
        window[slot, history:, :] = friction_solve(drive, friction)

    if slots <= 8:
        for slot in range(slots):
            one_slot(slot)
    else:
        pl.loop(0, slots)(one_slot)
    convolve_and_route(
        window, stacked, responses, sums, early, late, late_copy, table, table_copy, totals
    )
    rates_tail_ref[...] = window[:, BLOCK:, :]
    responses_tail_ref[...] = responses[:, :, BLOCK:, :]


def next_stress_kernel(
    table_ref, rates_ref, rates_tail_ref, responses_tail_ref, early, late,
    *refs,
):
    totals, (window, stacked, responses, table, table_sem, *sums) = refs[:4], refs[4:]
    table_copy = pltpu.make_async_copy(table_ref, table, table_sem)
    table_copy.start()
    history = window.shape[1] - BLOCK
    window[:, :history, :] = rates_tail_ref[...]
    window[:, history:, :] = rates_ref[...]
    responses[:, :, :history, :] = responses_tail_ref[...]
    convolve_and_route(
        window, stacked, responses, sums, early, late, None, table, table_copy, totals
    )


def solve_patch(
    block_idx, patch, first, prestress_ref, friction_ref, load_ref, kept_ref, came_ref
):
    width = prestress_ref.shape[1]
    row = pl.ds(first + patch, 1)
    stress = kept_ref[0, patch] + came_ref[0, patch]
    drive = prestress_ref[row, :] + load_ref[row, :] * times_of(block_idx, width) + stress
    return friction_solve(drive, jnp.broadcast_to(friction_ref[row, :], drive.shape))


def solve_group_kernel(
    block_idx, prestress_ref, friction_ref, load_ref, kept_ref, came_ref, rates_ref
):
    for patch in range(rates_ref.shape[0]):
        rates_ref[patch] = solve_patch(
            block_idx, patch, 0, prestress_ref, friction_ref, load_ref, kept_ref, came_ref
        )


def middle_block_kernel(
    received_ref, prestress_ref, friction_ref, load_ref, kept_ref, came_ref, others_ref,
    rates_ref, outgoing_ref,
):
    known = others_ref.shape[0]
    rates_ref[:known] = others_ref[...]
    for patch in range(rates_ref.shape[0] - known):
        rates_ref[known + patch] = solve_patch(
            1, patch, known, prestress_ref, friction_ref, load_ref, kept_ref, came_ref
        )

    asked_row = received_ref.shape[1] - 1

    def one_slot(slot):
        asked = jnp.broadcast_to(received_ref[slot, asked_row:, :], outgoing_ref.shape[1:])
        chosen = rates_ref[0]
        for patch in range(1, rates_ref.shape[0]):
            chosen = jnp.where(asked == patch, rates_ref[patch], chosen)
        outgoing_ref[slot] = chosen

    slots = outgoing_ref.shape[0]
    if slots <= 8:
        for slot in range(slots):
            one_slot(slot)
    else:
        pl.loop(0, slots)(one_slot)


def last_block_kernel(
    prestress_ref, friction_ref, load_ref, kept_ref, came_ref, others_ref, begun_ref, out_ref,
    rates, sems,
):
    known, patches = others_ref.shape[0], rates.shape[0]
    copies = [
        pltpu.make_async_copy(
            rates.at[patch], out_ref.at[known + patch, 2 * BLOCK :], sems.at[patch]
        )
        for patch in range(patches)
    ]
    others = pltpu.make_async_copy(others_ref, out_ref.at[:known, 2 * BLOCK :], sems.at[patches])
    others.start()
    for patch in range(patches):
        rates[patch] = solve_patch(
            2, patch, known, prestress_ref, friction_ref, load_ref, kept_ref, came_ref
        )
        copies[patch].start()
    for copy in copies + [others]:
        copy.wait()


def local(interactions, list_lengths, kernels, prestress, friction, load_rate):
    n_recv = lax.axis_size("recv")
    n_src = lax.axis_size("src")
    ker_count, width, lag_count, _ = kernels.shape
    patch_count = prestress.shape[0]
    group_rows = n_src * patch_count
    bits = n_src.bit_length() - 1
    assert n_src == 1 << bits and bits > 0

    f32, bf16 = jnp.float32, jnp.bfloat16
    packed = pl.pallas_call(
        pack_kernel,
        in_specs=[VMEM] * 4,
        out_specs=VMEM,
        out_shape=jax.ShapeDtypeStruct((n_recv, 3 * patch_count + 1, width), f32),
        compiler_params=grant(2 + n_recv // 8),
        name="pack",
    )(*map(in_hbm, (interactions, prestress, friction, load_rate)))
    received = lax.all_to_all(packed, "recv", split_axis=0, concat_axis=0, tiled=True)

    late_lags = lag_count // 4
    early = jax.ShapeDtypeStruct((2 * ker_count, width, (lag_count - late_lags) * width), bf16)
    late_shape = (2 * ker_count, width, late_lags * width)
    late_halves = pltpu.VMEM(late_shape, bf16)
    kernels = in_hbm(kernels)
    early, late, table, wanted = pl.pallas_call(
        functools.partial(prepare_kernel, patch_count),
        in_specs=[HBM] * 3,
        out_specs=[VMEM, HBM, VMEM, VMEM],
        out_shape=[
            early,
            jax.ShapeDtypeStruct((24 * ker_count,) + late_shape[1:], bf16),
            jax.ShapeDtypeStruct((2, interactions.shape[1]), jnp.int32),
            jax.ShapeDtypeStruct((n_recv, width), f32),
        ],
        scratch_shapes=[
            pltpu.VMEM(interactions.shape, jnp.int32),
            pltpu.SMEM(list_lengths.shape, jnp.int32),
            pltpu.VMEM((ker_count, width, lag_count + PAD, width), f32),
            late_halves,
            pltpu.SemaphoreType.DMA((2,)),
            pltpu.SemaphoreType.DMA((ker_count,)),
            pltpu.SemaphoreType.DMA((2 * ker_count,)),
        ],
        compiler_params=grant(46),
        name="prepare",
    )(list_lengths, in_hbm(interactions), kernels)
    late_shape, late = jax.ShapeDtypeStruct(late_shape, bf16), in_hbm(late)
    last_patches = patch_count // 4
    group_sizes = patch_count - last_patches, last_patches
    halves = [
        jax.ShapeDtypeStruct((n_src // 2, size, BLOCK, width), f32)
        for size in group_sizes
        for part in range(2)
    ]
    rates_tail = jax.ShapeDtypeStruct((n_recv, lag_count, width), f32)
    responses_tail = jax.ShapeDtypeStruct((ker_count, n_recv, lag_count, width), f32)
    chunk = min(8, n_recv)
    stress_mib = 16 + 8 * ker_count * n_recv * (lag_count + BLOCK) * width // 2**20
    scratch = [
        pltpu.VMEM((n_recv, lag_count + BLOCK, width), f32),
        pltpu.VMEM((2 * chunk * BLOCK, lag_count * width), bf16),
        pltpu.VMEM((ker_count, n_recv, lag_count + BLOCK, width), f32),
        pltpu.SMEM((2, interactions.shape[1]), jnp.int32),
        pltpu.SemaphoreType.DMA,
    ] + [pltpu.VMEM(((group_rows + 1) * BLOCK, width), f32)] * 2

    def reduce_scatter(kept, sent):
        for bit in range(bits):
            pairs = [(i, i ^ (1 << bit)) for i in range(n_src)]
            came = lax.ppermute(sent, "src", pairs)
            if bit == bits - 1:
                return kept, came
            quarter = kept.shape[0] // 2
            sent = kept[quarter:] + came[quarter:]
            kept = kept[:quarter] + came[:quarter]

    rates_group = jax.ShapeDtypeStruct((group_sizes[0], BLOCK, width), f32)

    def solve_first_group(block_idx, terms):
        return pl.pallas_call(
            functools.partial(solve_group_kernel, block_idx),
            in_specs=[VMEM] * 5,
            out_specs=VMEM,
            out_shape=rates_group,
            compiler_params=grant(2),
            name="solve_group",
        )(prestress, friction, load_rate, *terms)

    *totals, rates_tail, responses_tail, late = pl.pallas_call(
        first_stress_kernel,
        in_specs=[VMEM] * 4 + [HBM],
        out_specs=[VMEM] * 7,
        out_shape=halves + [rates_tail, responses_tail, late_shape],
        scratch_shapes=scratch[:3] + [pltpu.SemaphoreType.DMA] + scratch[3:],
        compiler_params=grant(stress_mib),
        name="first_stress",
    )(table, wanted, received, early, late)
    terms = [reduce_scatter(*totals[:2]), reduce_scatter(*totals[2:])]
    second_rates, outgoing = pl.pallas_call(
        middle_block_kernel,
        in_specs=[VMEM] * 7,
        out_specs=[VMEM] * 2,
        out_shape=[
            jax.ShapeDtypeStruct((patch_count, BLOCK, width), f32),
            jax.ShapeDtypeStruct((n_recv, BLOCK, width), f32),
        ],
        compiler_params=grant(4),
        name="middle_block",
    )(received, prestress, friction, load_rate, *terms[1], solve_first_group(1, terms[0]))
    rates = lax.all_to_all(outgoing, "recv", split_axis=0, concat_axis=0, tiled=True)
    totals = pl.pallas_call(
        next_stress_kernel,
        in_specs=[VMEM] * 6,
        out_specs=[VMEM] * 4,
        out_shape=halves,
        scratch_shapes=scratch,
        compiler_params=grant(stress_mib),
        name="next_stress",
    )(table, rates, rates_tail, responses_tail, early, late)
    terms = [reduce_scatter(*totals[:2]), reduce_scatter(*totals[2:])]
    output = pl.pallas_call(
        first_blocks_kernel,
        in_specs=[VMEM] * 4,
        out_specs=HBM,
        out_shape=jax.ShapeDtypeStruct((patch_count, BLOCKS * BLOCK, width), f32),
        scratch_shapes=[
            pltpu.VMEM((patch_count, BLOCK, width), f32),
            pltpu.SemaphoreType.DMA((2,)),
        ],
        compiler_params=grant(4),
        name="first_blocks",
    )(prestress, friction, load_rate, second_rates)
    return pl.pallas_call(
        last_block_kernel,
        in_specs=[VMEM] * 6 + [HBM],
        out_specs=HBM,
        out_shape=jax.ShapeDtypeStruct(output.shape, f32),
        scratch_shapes=[
            pltpu.VMEM((last_patches, BLOCK, width), f32),
            pltpu.SemaphoreType.DMA((last_patches + 1,)),
        ],
        input_output_aliases={6: 0},
        compiler_params=grant(4),
        name="last_block",
    )(
        prestress, friction, load_rate, *terms[1], solve_first_group(2, terms[0]),
        output,
    )


def solution(mesh):
    in_specs = (
        P(None, ("recv", "src")),
        P(("recv", "src")),
        P(("recv", "src"), None, None, None),
        P(("recv", "src"), None),
        P(("recv", "src"), None),
        P(("recv", "src"), None),
    )
    out_specs = P(("recv", "src"), None, None)
    return jax.shard_map(local, mesh=mesh, in_specs=in_specs, out_specs=out_specs, check_vma=False)
```
